32 devices in a mesh: seq: 16 (over z, y, x), head: 2 (over core).
Axes of the slice: x: 2, y: 2, z: 4, core: 2. Of those that a mesh axis runs over, the one named last changes fastest.
Arguments:
- tokens: bfloat16 [4096, 768], P('seq', 'head'), may hold values from -6 to 6
- w_query: bfloat16 [768, 512], P(None, 'head'), may hold values from -0.21875 to 0.21875
- w_key: bfloat16 [768, 512], P(None, 'head'), may hold values from -0.21875 to 0.21875
- w_value: bfloat16 [768, 512], P(None, 'head'), may hold values from -0.21875 to 0.21875
- w_out: bfloat16 [512, 768], P('head'), may hold values from -0.25 to 0.25
- feature_dirs: float32 [64, 128], replicated, may hold values from -5 to 5
- kernel_taps: bfloat16 [8, 129], P('head'), may hold values from -0.3984375 to 0.3984375
Outputs:
- mixed: bfloat16 [4096, 768], P('seq', 'head')
- key_mixed: bfloat16 [4096, 512], P('seq', 'head')
The draws below stay inside these ranges and needn't reach their ends.
All inputs are finite; a program needn't handle non-finite values.
Results may differ from the reference program's by a relative error of at most 0.018.
Values may be sent and summed in bfloat16 or wider, within the bound.
A program may use at most 64 MiB of HBM per device.

```python
import jax
import jax.numpy as jnp
from jax import lax

D = 768
HEADS = 8
HEAD_DIM = 64
ATT = 512
FEATURES = 128
TAPS = 129
TOKENS = 4096


def levels(stream_key, dims, shards, low, largest):
    loudness, own = 1.0, jax.random.fold_in(stream_key, 6)
    for axis_at, blocks in shards:
        heights = jnp.exp(jax.random.uniform(jax.random.fold_in(own, axis_at), (blocks,), jnp.float32, low / len(shards), largest / len(shards)))
        loudness = loudness * jnp.repeat(heights, dims[axis_at] // blocks).reshape([-1 if axis == axis_at else 1 for axis in range(len(dims))])
    return loudness


def centred(rng, dims, spread, limit, pieces=(), held_as=jnp.bfloat16):
    values = spread * jax.random.normal(rng, dims, jnp.float32)
    if pieces:
        values = values * levels(rng, dims, pieces, -0.22, 0.18)
    return jnp.clip(values, -limit, limit).astype(held_as)


def setup_inputs(seed: int = 0) -> dict:
    seeds = jax.random.split(jax.random.key(seed), 8)
    return {
        "tokens": centred(seeds[0], (TOKENS, D), 1.0, 6.0, ((0, 16), (1, 2))),
        "w_query": centred(seeds[1], (D, ATT), D ** -0.5, 0.21875, ((1, 2),)),
        "w_key": centred(seeds[2], (D, ATT), D ** -0.5, 0.21875, ((1, 2),)),
        "w_value": centred(seeds[3], (D, ATT), D ** -0.5, 0.21875, ((1, 2),)),
        "w_out": centred(seeds[4], (ATT, D), ATT ** -0.5, 0.25, ((0, 2),)),
        "feature_dirs": centred(seeds[5], (HEAD_DIM, FEATURES), 1.0, 5.0, (), jnp.float32),
        "kernel_taps": centred(seeds[6], (HEADS, TAPS), 0.09, 0.3984375, ((0, 2),)),
    }


def build_band(taps, block):
    reach = (taps.shape[1] - 1) // 2
    width = block + 2 * reach
    padded_taps = jnp.pad(taps, ((0, 0), (0, width + 1 - taps.shape[1])))
    tiled = jnp.tile(padded_taps, (1, block))
    return tiled[:, :block * width].reshape(taps.shape[0], block, width)


def band_conv(keys_ext, band, blocks, block):
    span = band.shape[2]

    def one_block(index):
        window = lax.dynamic_slice_in_dim(keys_ext, index * block, span, 0)
        return jnp.einsum('hij,jhd->ihd', band, window.astype(jnp.float32), precision=lax.Precision.HIGHEST)

    result = lax.map(one_block, jnp.arange(blocks, dtype=jnp.int32))
    return result.reshape(blocks * block, keys_ext.shape[1], keys_ext.shape[2])


def reference(tokens, w_query, w_key, w_value, w_out, feature_dirs, kernel_taps):
    reach = (kernel_taps.shape[1] - 1) // 2
    block = min(512, TOKENS)
    key_scale = HEAD_DIM ** -0.25
    highest = lax.Precision.HIGHEST
    outputs = []
    key_outputs = []
    for head in range(HEADS):
        cols = slice(head * HEAD_DIM, (head + 1) * HEAD_DIM)
        queries = jnp.dot(tokens, w_query[:, cols], preferred_element_type=jnp.float32).astype(jnp.bfloat16)
        keys = jnp.dot(tokens, w_key[:, cols], preferred_element_type=jnp.float32).astype(jnp.bfloat16)
        values = jnp.dot(tokens, w_value[:, cols], preferred_element_type=jnp.float32).astype(jnp.bfloat16)
        padded = jnp.pad(keys, ((reach, reach), (0, 0)))[:, None, :]
        band = build_band(kernel_taps[head:head + 1], block).astype(jnp.float32)
        conv_keys = band_conv(padded, band, TOKENS // block, block)[:, 0, :]
        key_outputs.append(conv_keys.astype(jnp.bfloat16))
        scaled_keys = conv_keys * key_scale
        key_logits = jnp.dot(scaled_keys, feature_dirs, precision=highest)
        key_feats = jnp.exp(key_logits - 0.5 * jnp.sum(scaled_keys * scaled_keys, axis=1, keepdims=True)).astype(jnp.bfloat16)
        scaled_queries = queries.astype(jnp.float32) * key_scale
        query_feats = jnp.exp(jnp.dot(scaled_queries, feature_dirs, precision=highest)).astype(jnp.bfloat16)
        key_wide = key_feats.astype(jnp.float32)
        state = jnp.dot(key_wide.T, values.astype(jnp.float32), precision=highest)
        normal = jnp.sum(key_wide, axis=0)
        state_b = lax.optimization_barrier(state.astype(jnp.bfloat16)).astype(jnp.float32)
        normal_b = lax.optimization_barrier(normal.astype(jnp.bfloat16)).astype(jnp.float32)
        query_wide = query_feats.astype(jnp.float32)
        numer = jnp.dot(query_wide, state_b, precision=highest)
        denom = jnp.dot(query_wide, normal_b, precision=highest)
        outputs.append((numer / denom[:, None]).astype(jnp.bfloat16))
    attended = jnp.concatenate(outputs, axis=1)
    key_mixed = jnp.concatenate(key_outputs, axis=1)
    mixed = jnp.dot(attended, w_out, preferred_element_type=jnp.float32).astype(jnp.bfloat16)
    return (mixed, key_mixed)
```

```python
import functools

import jax
import jax.numpy as jnp
from jax import lax
from jax.experimental import pallas as pl
from jax.experimental.pallas import tpu as pltpu
from jax.sharding import PartitionSpec as P

HEAD_DIM = 64
LANES = 128
PAD = 16
MESH = pl.DeviceIdType.MESH
F32, BF16 = jnp.float32, jnp.bfloat16


def mm(a, b):
    return jnp.dot(a, b, preferred_element_type=F32)


def mm_nt(a, b):
    return lax.dot_general(a, b, (((1,), (1,)), ((), ())), preferred_element_type=F32)


def split(value):
    high = value.astype(BF16)
    return high, (value - high.astype(F32)).astype(BF16)


def fused(
    n, heads, reach, tok, wq, wk, wv, wo, dirs, taps, mixed, key_mixed,
    x, q_w, k_w, v_w, o_w, dirs_v, taps_v, taps_pad, band, dirs_hi, dirs_lo, norm_w,
    keys, conv, kmix, vt, queries, qf, part, part_b, inner_in, outer_b, outer_in, full, gate, att, out_v,
    loc, send, recv, inner_send, inner_recv, outer_send, outer_recv, full_send, full_recv,
):
    rows, half = tok.shape
    features = dirs.shape[1]
    out_cols = mixed.shape[1]
    width = heads * HEAD_DIM
    pairs = width // LANES
    group, block = heads, 2 * reach
    outer = n // group
    scale = HEAD_DIM ** (-0.25)
    me, core = lax.axis_index("seq"), lax.axis_index("head")
    other = 1 - core
    spot, plane = lax.rem(me, group), lax.div(me, group)

    def inner_peer(d):
        return plane * group + lax.rem(spot + d, group)

    def outer_peer(e):
        return lax.rem(plane + e, outer) * group + spot

    barrier = pltpu.get_barrier_semaphore()

    def greet(seq_id, core_id):
        pl.semaphore_signal(barrier, inc=1, device_id=(seq_id, core_id), device_id_type=MESH)

    for e in range(1, outer):
        greet(outer_peer(e), core)

    @pl.when(me > 0)
    def _():
        greet(me - 1, core)
        greet(me - 1, other)

    @pl.when(me < n - 1)
    def _():
        greet(me + 1, core)
        greet(me + 1, other)

    for d in range(1, group):
        greet(inner_peer(d), core)
    greet(me, other)

    own_cols = pl.ds(pl.multiple_of(core * half, LANES), half)
    main = pl.ds(reach, rows)
    my_out = pl.ds(pl.multiple_of(core * out_cols, LANES), out_cols)
    other_out = pl.ds(pl.multiple_of(other * out_cols, LANES), out_cols)
    local = [
        pltpu.make_async_copy(src, dst, loc.at[at])
        for at, (src, dst) in enumerate(
            [
                (tok, x.at[main, own_cols]),
                (wk, k_w),
                (wv, v_w),
                (dirs, dirs_v),
                (taps, taps_v),
                (wq, q_w),
                (wo.at[:, my_out], o_w.at[core]),
            ]
        )
    ]
    for copy in local:
        copy.start()

    @pl.when(me == 0)
    def _():
        x[0:reach, :] = jnp.zeros((reach, x.shape[1]), BF16)

    @pl.when(me == n - 1)
    def _():
        x[reach + rows :, :] = jnp.zeros((reach, x.shape[1]), BF16)

    sides = 2 * ((me > 0).astype(jnp.int32) + (me < n - 1).astype(jnp.int32))
    pl.semaphore_wait(barrier, outer - 1 + group + sides)

    def remote(src, dst, at, seq_id, core_id):
        return pltpu.make_async_remote_copy(
            src_ref=src, dst_ref=dst, send_sem=send.at[at], recv_sem=recv.at[at],
            device_id=(seq_id, core_id), device_id_type=MESH,
        )

    swap_tok = remote(tok, x.at[main, own_cols], 0, me, other)
    lower = [
        remote(tok.at[pl.ds(0, reach), :], x.at[pl.ds(reach + rows, reach), own_cols], 1 + k, me - 1, c)
        for k, c in enumerate((core, other))
    ]
    upper = [
        remote(tok.at[pl.ds(rows - reach, reach), :], x.at[pl.ds(0, reach), own_cols], 3 + k, me + 1, c)
        for k, c in enumerate((core, other))
    ]
    swap_out = remote(wo.at[:, other_out], o_w.at[core], 5, me, other)

    @pl.when(me > 0)
    def _():
        for copy in lower:
            copy.start()

    @pl.when(me < n - 1)
    def _():
        for copy in upper:
            copy.start()

    swap_tok.start()
    swap_out.start()

    dirs_hi[...] = jnp.zeros(dirs_hi.shape, BF16)
    dirs_lo[...] = jnp.zeros(dirs_lo.shape, BF16)
    norm_w[...] = jnp.zeros(norm_w.shape, BF16)
    gate[...] = jnp.zeros(gate.shape, BF16)
    taps_pad[...] = jnp.zeros(taps_pad.shape, F32)
    for h in range(heads):
        r, c = slice(h * HEAD_DIM, (h + 1) * HEAD_DIM), slice(h * features, (h + 1) * features)
        norm_w[r, c] = jnp.full((HEAD_DIM, features), 0.5 * HEAD_DIM ** (-0.5), BF16)
        vt[h, HEAD_DIM:, :] = jnp.ones((PAD, rows), BF16)
    local[3].wait()
    dir_high, dir_low = split(dirs_v[...] * scale)
    for h in range(heads):
        r, c = slice(h * HEAD_DIM, (h + 1) * HEAD_DIM), slice(h * features, (h + 1) * features)
        dirs_hi[r, c] = dir_high
        dirs_lo[r, c] = dir_low
    local[4].wait()
    taps_pad[0:heads, 0 : block + 1] = taps_v[...].astype(F32)
    for h in range(heads):
        row = jnp.broadcast_to(taps_pad[h : h + 1, :], (block, 2 * block))
        band[h * block : (h + 1) * block, :] = pltpu.roll(row, 0, 1, stride=1, stride_axis=0).astype(BF16)

    local[0].wait()
    local[1].wait()
    swap_tok.wait_recv()
    keys[reach : reach + rows, :] = mm(x[reach : reach + rows, :], k_w[...]).astype(BF16)
    local[2].wait()
    values_t = mm(x[reach : reach + rows, :], v_w[...]).T.astype(BF16)
    for h in range(heads):
        vt[h, 0:HEAD_DIM, :] = values_t[h * HEAD_DIM : (h + 1) * HEAD_DIM, :]

    @pl.when(me > 0)
    def _():
        for copy in upper:
            copy.wait_recv()

    @pl.when(me < n - 1)
    def _():
        for copy in lower:
            copy.wait_recv()

    keys[0:reach, :] = mm(x[0:reach, :], k_w[...]).astype(BF16)
    keys[reach + rows :, :] = mm(x[reach + rows :, :], k_w[...]).astype(BF16)

    lane = lax.broadcasted_iota(jnp.int32, (block, LANES), 1)
    for b in range(rows // block):
        for p in range(pairs):
            got = mm(
                band[2 * p * block : 2 * (p + 1) * block, :],
                keys[b * block : (b + 2) * block, p * LANES : (p + 1) * LANES],
            )
            conv[b * block : (b + 1) * block, p * LANES : (p + 1) * LANES] = jnp.where(
                lane < HEAD_DIM, got[:block], got[block:]
            )
    c = conv[...]
    c_hi, c_lo = split(c)
    kmix[...] = c_hi
    sq_hi, sq_lo = split(c * c)
    out_keys = pltpu.make_async_copy(kmix, key_mixed, loc.at[7])
    out_keys.start()
    logits = mm(c_hi, dirs_hi[...]) + mm(c_lo, dirs_hi[...]) + mm(c_hi, dirs_lo[...])
    logits = logits - (mm(sq_hi, norm_w[...]) + mm(sq_lo, norm_w[...]))
    kf = jnp.exp(logits).astype(BF16)
    for h in range(heads):
        got = mm(vt[h], kf[:, h * features : (h + 1) * features])
        part[h] = got
        part_b[h] = got.astype(BF16)

    scatter = [
        pltpu.make_async_remote_copy(
            src_ref=part_b.at[lax.rem(spot + d, group)], dst_ref=inner_in.at[d - 1],
            send_sem=inner_send.at[d - 1], recv_sem=inner_recv.at[d - 1],
            device_id=(inner_peer(d), core), device_id_type=MESH,
        )
        for d in range(1, group)
    ]
    for copy in scatter:
        copy.start()
    local[5].wait()
    queries[...] = mm(x[reach : reach + rows, :], q_w[...]).astype(BF16)
    mine = part[spot]
    for d in range(1, group):
        scatter[d - 1].wait_recv()
        mine = mine + inner_in[d - 1].astype(F32)
    outer_b[...] = mine.astype(BF16)
    spread = [
        pltpu.make_async_remote_copy(
            src_ref=outer_b, dst_ref=outer_in.at[e - 1],
            send_sem=outer_send.at[e - 1], recv_sem=outer_recv.at[e - 1],
            device_id=(outer_peer(e), core), device_id_type=MESH,
        )
        for e in range(1, outer)
    ]
    for copy in spread:
        copy.start()
    q = queries[...]
    qf[...] = jnp.exp(mm(q, dirs_hi[...]) + mm(q, dirs_lo[...])).astype(BF16)
    for e in range(1, outer):
        spread[e - 1].wait_recv()
        mine = mine + outer_in[e - 1].astype(F32)
    full[spot] = mine.astype(BF16)
    gather = [
        pltpu.make_async_remote_copy(
            src_ref=full.at[spot], dst_ref=full.at[spot],
            send_sem=full_send.at[d - 1], recv_sem=full_recv.at[d - 1],
            device_id=(inner_peer(d), core), device_id_type=MESH,
        )
        for d in range(1, group)
    ]
    for copy in gather:
        copy.start()
    for copy in gather:
        copy.wait_recv()

    for h in range(heads):
        p, k = divmod(h, 2)
        r = slice(k * HEAD_DIM, (k + 1) * HEAD_DIM)
        s = slice(LANES + k * HEAD_DIM, LANES + (k + 1) * HEAD_DIM)
        f = slice(k * features, (k + 1) * features)
        gate[p, r, f] = full[h, 0:HEAD_DIM, :]
        gate[p, s, f] = jnp.concatenate([full[h, HEAD_DIM:, :]] * (HEAD_DIM // PAD), axis=0)
    steps = 2
    span = rows // steps
    swap_att = []
    for b in range(steps):
        r = slice(b * span, (b + 1) * span)
        for p in range(pairs):
            got = mm_nt(qf[r, 2 * p * features : 2 * (p + 1) * features], gate[p])
            att[core, r, p * LANES : (p + 1) * LANES] = (got[:, :LANES] / got[:, LANES:]).astype(BF16)
        piece = att.at[core, pl.ds(b * span, span), :]
        copy = remote(piece, piece, 6 + b, me, other)
        copy.start()
        swap_att.append(copy)
    local[6].wait()
    own = [mm(att[core, b * span : (b + 1) * span, :], o_w[core]) for b in range(steps)]
    swap_out.wait_recv()
    outs = []
    for b in range(steps):
        r = slice(b * span, (b + 1) * span)
        swap_att[b].wait_recv()
        out_v[r, :] = (own[b] + mm(att[other, r, :], o_w[other])).astype(BF16)
        copy = pltpu.make_async_copy(
            out_v.at[pl.ds(b * span, span), :], mixed.at[pl.ds(b * span, span), :], loc.at[8 + b]
        )
        copy.start()
        outs.append(copy)

    for copy in [swap_tok, swap_out] + scatter + spread + gather + swap_att:
        copy.wait_send()

    @pl.when(me > 0)
    def _():
        for copy in lower:
            copy.wait_send()

    @pl.when(me < n - 1)
    def _():
        for copy in upper:
            copy.wait_send()

    out_keys.wait()
    for copy in outs:
        copy.wait()


def body(n, tokens, w_query, w_key, w_value, w_out, feature_dirs, kernel_taps):
    rows, half = tokens.shape
    d = w_key.shape[0]
    width = w_key.shape[1]
    heads = width // HEAD_DIM
    features = feature_dirs.shape[1]
    reach = (kernel_taps.shape[1] - 1) // 2
    block = 2 * reach
    out_cols = w_out.shape[1] // 2
    outer = n // heads
    chunk = HEAD_DIM + PAD
    vmem = pltpu.VMEM
    dma = pltpu.SemaphoreType.DMA
    any_spec = pl.BlockSpec(memory_space=pl.ANY)
    return pl.pallas_call(
        functools.partial(fused, n, heads, reach),
        out_shape=(
            jax.ShapeDtypeStruct((rows, out_cols), BF16),
            jax.ShapeDtypeStruct((rows, width), BF16),
        ),
        in_specs=[any_spec] * 7,
        out_specs=(any_spec, any_spec),
        scratch_shapes=[
            vmem((rows + 2 * reach, d), BF16),
            vmem((d, width), BF16),
            vmem((d, width), BF16),
            vmem((d, width), BF16),
            vmem((2, width, out_cols), BF16),
            vmem(feature_dirs.shape, F32),
            vmem(kernel_taps.shape, BF16),
            vmem((8, 2 * block), F32),
            vmem((heads * block, 2 * block), BF16),
            vmem((width, heads * features), BF16),
            vmem((width, heads * features), BF16),
            vmem((width, heads * features), BF16),
            vmem((rows + 2 * reach, width), BF16),
            vmem((rows, width), F32),
            vmem((rows, width), BF16),
            vmem((heads, chunk, rows), BF16),
            vmem((rows, width), BF16),
            vmem((rows, heads * features), BF16),
            vmem((heads, chunk, features), F32),
            vmem((heads, chunk, features), BF16),
            vmem((heads - 1, chunk, features), BF16),
            vmem((chunk, features), BF16),
            vmem((max(outer - 1, 1), chunk, features), BF16),
            vmem((heads, chunk, features), BF16),
            vmem((width // LANES, 2 * LANES, 2 * features), BF16),
            vmem((2, rows, width), BF16),
            vmem((rows, out_cols), BF16),
            dma((10,)),
            dma((8,)),
            dma((8,)),
            dma((heads - 1,)),
            dma((heads - 1,)),
            dma((max(outer - 1, 1),)),
            dma((max(outer - 1, 1),)),
            dma((heads - 1,)),
            dma((heads - 1,)),
        ],
        compiler_params=pltpu.CompilerParams(collective_id=0, has_side_effects=True),
        name="fused",
    )(tokens, w_query, w_key, w_value, w_out, feature_dirs, kernel_taps)


def solution(mesh):
    return jax.shard_map(
        functools.partial(body, mesh.shape["seq"]),
        mesh=mesh,
        in_specs=(
            P("seq", "head"),
            P(None, "head"),
            P(None, "head"),
            P(None, "head"),
            P("head", None),
            P(),
            P("head", None),
        ),
        out_specs=(P("seq", "head"), P("seq", "head")),
        check_vma=False,
    )
```

```python
import functools

import jax
import jax.numpy as jnp
from jax import lax
from jax.experimental import pallas as pl
from jax.experimental.pallas import tpu as pltpu
from jax.sharding import PartitionSpec as P

HEAD_DIM = 64
LANES = 128
PAD = 8
MESH = pl.DeviceIdType.MESH
F32, BF16 = jnp.float32, jnp.bfloat16


def mm(a, b):
    return jnp.dot(a, b, preferred_element_type=F32)


def mm_nt(a, b):
    return lax.dot_general(a, b, (((1,), (1,)), ((), ())), preferred_element_type=F32)


def split(value):
    high = value.astype(BF16)
    return high, (value - high.astype(F32)).astype(BF16)


def fused(
    n, heads, reach, tok, wq, wk, wv, wo, dirs, taps, part_out, att_in, o_w_in, kmix,
    x, q_w, k_w, v_w, o_w, dirs_v, taps_v, taps_pad, band, dirs_hi, dirs_lo, norm_w,
    keys, conv, vt, queries, qf, part, part_b, inner_in, outer_b, outer_in, full, gate, att,
    loc, send, recv, inner_send, inner_recv, outer_send, outer_recv, full_send, full_recv,
):
    rows, half = tok.shape
    features = dirs.shape[1]
    out_cols = part_out.shape[1]
    width = heads * HEAD_DIM
    pairs = width // LANES
    group, block = heads, 2 * reach
    outer = n // group
    scale = HEAD_DIM ** (-0.25)
    me, core = lax.axis_index("seq"), lax.axis_index("head")
    other = 1 - core
    spot, plane = lax.rem(me, group), lax.div(me, group)

    def inner_peer(d):
        return plane * group + lax.rem(spot + d, group)

    def outer_peer(e):
        return lax.rem(plane + e, outer) * group + spot

    barrier = pltpu.get_barrier_semaphore()

    def greet(seq_id, core_id):
        pl.semaphore_signal(barrier, inc=1, device_id=(seq_id, core_id), device_id_type=MESH)

    for e in range(1, outer):
        greet(outer_peer(e), core)

    @pl.when(me > 0)
    def _():
        greet(me - 1, core)

    @pl.when(me < n - 1)
    def _():
        greet(me + 1, core)

    for d in range(1, group):
        greet(inner_peer(d), core)
    greet(me, other)

    own_cols = pl.ds(pl.multiple_of(core * half, LANES), half)
    main = pl.ds(reach, rows)
    my_out = pl.ds(pl.multiple_of(core * out_cols, LANES), out_cols)
    other_out = pl.ds(pl.multiple_of(other * out_cols, LANES), out_cols)
    local = [
        pltpu.make_async_copy(src, dst, loc.at[at])
        for at, (src, dst) in enumerate(
            [
                (tok, x.at[main, own_cols]),
                (wk, k_w),
                (wv, v_w),
                (dirs, dirs_v),
                (taps, taps_v),
                (wq, q_w),
                (wo.at[:, my_out], o_w),
            ]
        )
    ]
    for copy in local:
        copy.start()

    @pl.when(me == 0)
    def _():
        x[0:reach, :] = jnp.zeros((reach, x.shape[1]), BF16)

    @pl.when(me == n - 1)
    def _():
        x[reach + rows :, :] = jnp.zeros((reach, x.shape[1]), BF16)

    sides = ((me > 0).astype(jnp.int32) + (me < n - 1).astype(jnp.int32))
    pl.semaphore_wait(barrier, outer - 1 + group + sides)

    def remote(src, dst, at, seq_id, core_id):
        return pltpu.make_async_remote_copy(
            src_ref=src, dst_ref=dst, send_sem=send.at[at], recv_sem=recv.at[at],
            device_id=(seq_id, core_id), device_id_type=MESH,
        )

    swap_tok = remote(tok, x.at[main, own_cols], 0, me, other)
    pieces = 2
    part_rows = reach // pieces
    lower, upper, lower_on, upper_on = [], [], [], []
    for k in range(pieces):
        low = x.at[pl.ds(reach + rows + k * part_rows, part_rows), own_cols]
        high = x.at[pl.ds(k * part_rows, part_rows), own_cols]
        lower.append(remote(tok.at[pl.ds(k * part_rows, part_rows), :], low, 4 + k, me - 1, core))
        upper.append(
            remote(tok.at[pl.ds(rows - reach + k * part_rows, part_rows), :], high, 6 + k, me + 1, core)
        )
        lower_on.append(remote(low, low, 8 + k, me, other))
        upper_on.append(remote(high, high, 10 + k, me, other))
    swap_out = remote(wo.at[:, other_out], o_w_in, 1, me, other)

    @pl.when(me > 0)
    def _():
        for copy in lower:
            copy.start()

    @pl.when(me < n - 1)
    def _():
        for copy in upper:
            copy.start()

    swap_tok.start()

    dirs_hi[...] = jnp.zeros(dirs_hi.shape, BF16)
    dirs_lo[...] = jnp.zeros(dirs_lo.shape, BF16)
    norm_w[...] = jnp.zeros(norm_w.shape, BF16)
    gate[...] = jnp.zeros(gate.shape, BF16)
    taps_pad[...] = jnp.zeros(taps_pad.shape, F32)
    for h in range(heads):
        r, c = slice(h * HEAD_DIM, (h + 1) * HEAD_DIM), slice(h * features, (h + 1) * features)
        norm_w[r, c] = jnp.full((HEAD_DIM, features), 0.5 * HEAD_DIM ** (-0.5), BF16)
        vt[h, HEAD_DIM:, :] = jnp.ones((PAD, rows), BF16)
    local[3].wait()
    dir_high, dir_low = split(dirs_v[...] * scale)
    for h in range(heads):
        r, c = slice(h * HEAD_DIM, (h + 1) * HEAD_DIM), slice(h * features, (h + 1) * features)
        dirs_hi[r, c] = dir_high
        dirs_lo[r, c] = dir_low
    local[4].wait()
    taps_pad[0:heads, 0 : block + 1] = taps_v[...].astype(F32)
    for h in range(heads):
        row = jnp.broadcast_to(taps_pad[h : h + 1, :], (block, 2 * block))
        band[h * block : (h + 1) * block, :] = pltpu.roll(row, 0, 1, stride=1, stride_axis=0).astype(BF16)

    local[0].wait()
    local[1].wait()
    swap_tok.wait_recv()
    keys[reach : reach + rows, :] = mm(x[reach : reach + rows, :], k_w[...]).astype(BF16)
    local[2].wait()
    values_t = mm(x[reach : reach + rows, :], v_w[...]).T.astype(BF16)
    for h in range(heads):
        vt[h, 0:HEAD_DIM, :] = values_t[h * HEAD_DIM : (h + 1) * HEAD_DIM, :]

    @pl.when(me > 0)
    def _():
        for copy, on in zip(upper, upper_on):
            copy.wait_recv()
            on.start()

    @pl.when(me < n - 1)
    def _():
        for copy, on in zip(lower, lower_on):
            copy.wait_recv()
            on.start()

    @pl.when(me > 0)
    def _():
        for on in upper_on:
            on.wait_recv()

    @pl.when(me < n - 1)
    def _():
        for on in lower_on:
            on.wait_recv()

    keys[0:reach, :] = mm(x[0:reach, :], k_w[...]).astype(BF16)
    keys[reach + rows :, :] = mm(x[reach + rows :, :], k_w[...]).astype(BF16)

    lane = lax.broadcasted_iota(jnp.int32, (block, LANES), 1)
    for b in range(rows // block):
        for p in range(pairs):
            got = mm(
                band[2 * p * block : 2 * (p + 1) * block, :],
                keys[b * block : (b + 2) * block, p * LANES : (p + 1) * LANES],
            )
            conv[b * block : (b + 1) * block, p * LANES : (p + 1) * LANES] = jnp.where(
                lane < HEAD_DIM, got[:block], got[block:]
            )
    c = conv[...]
    c_hi, c_lo = split(c)
    kmix[...] = c_hi
    sq_hi, sq_lo = split(c * c)
    logits = mm(c_hi, dirs_hi[...]) + mm(c_lo, dirs_hi[...]) + mm(c_hi, dirs_lo[...])
    logits = logits - (mm(sq_hi, norm_w[...]) + mm(sq_lo, norm_w[...]))
    kf = jnp.exp(logits).astype(BF16)
    for h in range(heads):
        got = mm(vt[h], kf[:, h * features : (h + 1) * features])
        part[h] = got
        part_b[h] = got.astype(BF16)

    scatter = [
        pltpu.make_async_remote_copy(
            src_ref=part_b.at[lax.rem(spot + d, group)], dst_ref=inner_in.at[d - 1],
            send_sem=inner_send.at[d - 1], recv_sem=inner_recv.at[d - 1],
            device_id=(inner_peer(d), core), device_id_type=MESH,
        )
        for d in range(1, group)
    ]
    for copy in scatter:
        copy.start()
    swap_out.start()
    local[5].wait()
    queries[...] = mm(x[reach : reach + rows, :], q_w[...]).astype(BF16)
    mine = part[spot]
    for d in range(1, group):
        scatter[d - 1].wait_recv()
        mine = mine + inner_in[d - 1].astype(F32)
    outer_b[...] = mine.astype(BF16)
    spread = [
        pltpu.make_async_remote_copy(
            src_ref=outer_b, dst_ref=outer_in.at[e - 1],
            send_sem=outer_send.at[e - 1], recv_sem=outer_recv.at[e - 1],
            device_id=(outer_peer(e), core), device_id_type=MESH,
        )
        for e in range(1, outer)
    ]
    for copy in spread:
        copy.start()
    q = queries[...]
    qf[...] = jnp.exp(mm(q, dirs_hi[...]) + mm(q, dirs_lo[...])).astype(BF16)
    for e in range(1, outer):
        spread[e - 1].wait_recv()
        mine = mine + outer_in[e - 1].astype(F32)
    full[spot] = mine.astype(BF16)
    gather = [
        pltpu.make_async_remote_copy(
            src_ref=full.at[spot], dst_ref=full.at[spot],
            send_sem=full_send.at[d - 1], recv_sem=full_recv.at[d - 1],
            device_id=(inner_peer(d), core), device_id_type=MESH,
        )
        for d in range(1, group)
    ]
    for copy in gather:
        copy.start()
    for copy in gather:
        copy.wait_recv()

    for h in range(heads):
        p, k = divmod(h, 2)
        r = slice(k * HEAD_DIM, (k + 1) * HEAD_DIM)
        s = slice(LANES + k * HEAD_DIM, LANES + (k + 1) * HEAD_DIM)
        f = slice(k * features, (k + 1) * features)
        gate[p, r, f] = full[h, 0:HEAD_DIM, :]
        gate[p, s, f] = jnp.broadcast_to(full[h, HEAD_DIM : HEAD_DIM + 1, :], (HEAD_DIM, features))
    steps = 2
    span = rows // steps
    swap_att = []
    for b in range(steps):
        r = slice(b * span, (b + 1) * span)
        for p in range(pairs):
            got = mm_nt(qf[r, 2 * p * features : 2 * (p + 1) * features], gate[p])
            att[r, p * LANES : (p + 1) * LANES] = (got[:, :LANES] / got[:, LANES:]).astype(BF16)
        piece = pl.ds(b * span, span)
        copy = remote(att.at[piece, :], att_in.at[piece, :], 2 + b, me, other)
        copy.start()
        swap_att.append(copy)
    local[6].wait()
    part_out[...] = mm(att[...], o_w[...])
    swap_out.wait_recv()
    for copy in swap_att:
        copy.wait_recv()
    for copy in [swap_tok, swap_out] + scatter + spread + gather + swap_att:
        copy.wait_send()

    @pl.when(me > 0)
    def _():
        for copy in lower + upper_on:
            copy.wait_send()

    @pl.when(me < n - 1)
    def _():
        for copy in upper + lower_on:
            copy.wait_send()


def finish(part_in, att_in, o_w_in, kmix, mixed, key_mixed, out_v, sem):
    rows = att_in.shape[0]
    out_keys = pltpu.make_async_copy(kmix, key_mixed, sem.at[0])
    out_keys.start()
    outs = []
    steps = 2
    span = rows // steps
    for b in range(steps):
        r = slice(b * span, (b + 1) * span)
        out_v[r, :] = (part_in[r, :] + mm(att_in[r, :], o_w_in[...])).astype(BF16)
        piece = pl.ds(b * span, span)
        outs.append(pltpu.make_async_copy(out_v.at[piece, :], mixed.at[piece, :], sem.at[1 + b]))
        outs[b].start()
    out_keys.wait()
    for copy in outs:
        copy.wait()


def body(n, tokens, w_query, w_key, w_value, w_out, feature_dirs, kernel_taps):
    rows, half = tokens.shape
    d = w_key.shape[0]
    width = w_key.shape[1]
    heads = width // HEAD_DIM
    features = feature_dirs.shape[1]
    reach = (kernel_taps.shape[1] - 1) // 2
    block = 2 * reach
    out_cols = w_out.shape[1] // 2
    outer = n // heads
    chunk = HEAD_DIM + PAD
    vmem = pltpu.VMEM
    dma = pltpu.SemaphoreType.DMA
    any_spec = pl.BlockSpec(memory_space=pl.ANY)
    vmem_spec = pl.BlockSpec(memory_space=pltpu.VMEM)
    held = pl.pallas_call(
        functools.partial(fused, n, heads, reach),
        out_shape=(
            vmem((rows, out_cols), F32),
            vmem((rows, width), BF16),
            vmem((width, out_cols), BF16),
            vmem((rows, width), BF16),
        ),
        in_specs=[any_spec] * 7,
        out_specs=(vmem_spec,) * 4,
        scratch_shapes=[
            vmem((rows + 2 * reach, d), BF16),
            vmem((d, width), BF16),
            vmem((d, width), BF16),
            vmem((d, width), BF16),
            vmem((width, out_cols), BF16),
            vmem(feature_dirs.shape, F32),
            vmem(kernel_taps.shape, BF16),
            vmem((8, 2 * block), F32),
            vmem((heads * block, 2 * block), BF16),
            vmem((width, heads * features), BF16),
            vmem((width, heads * features), BF16),
            vmem((width, heads * features), BF16),
            vmem((rows + 2 * reach, width), BF16),
            vmem((rows, width), F32),
            vmem((heads, chunk, rows), BF16),
            vmem((rows, width), BF16),
            vmem((rows, heads * features), BF16),
            vmem((heads, chunk, features), F32),
            vmem((heads, chunk, features), BF16),
            vmem((heads - 1, chunk, features), BF16),
            vmem((chunk, features), BF16),
            vmem((max(outer - 1, 1), chunk, features), BF16),
            vmem((heads, chunk, features), BF16),
            vmem((width // LANES, 2 * LANES, 2 * features), BF16),
            vmem((rows, width), BF16),
            dma((7,)),
            dma((12,)),
            dma((12,)),
            dma((heads - 1,)),
            dma((heads - 1,)),
            dma((max(outer - 1, 1),)),
            dma((max(outer - 1, 1),)),
            dma((heads - 1,)),
            dma((heads - 1,)),
        ],
        compiler_params=pltpu.CompilerParams(collective_id=0, has_side_effects=True),
        name="fused",
    )(tokens, w_query, w_key, w_value, w_out, feature_dirs, kernel_taps)
    return pl.pallas_call(
        finish,
        out_shape=(
            jax.ShapeDtypeStruct((rows, out_cols), BF16),
            jax.ShapeDtypeStruct((rows, width), BF16),
        ),
        in_specs=[vmem_spec] * 4,
        out_specs=(any_spec, any_spec),
        scratch_shapes=[vmem((rows, out_cols), BF16), dma((3,))],
        name="finish",
    )(*[pltpu.with_memory_space_constraint(a, pltpu.VMEM) for a in held])


def solution(mesh):
    return jax.shard_map(
        functools.partial(body, mesh.shape["seq"]),
        mesh=mesh,
        in_specs=(
            P("seq", "head"),
            P(None, "head"),
            P(None, "head"),
            P(None, "head"),
            P("head", None),
            P(),
            P("head", None),
        ),
        out_specs=(P("seq", "head"), P("seq", "head")),
        check_vma=False,
    )
```

```python
import functools

import jax
import jax.numpy as jnp
from jax import lax
from jax.experimental import pallas as pl
from jax.experimental.pallas import tpu as pltpu
from jax.sharding import PartitionSpec as P

HEAD_DIM = 64
LANES = 128
PAD = 8
MESH = pl.DeviceIdType.MESH
F32, BF16 = jnp.float32, jnp.bfloat16


def mm(a, b):
    return jnp.dot(a, b, preferred_element_type=F32)


def mm_nt(a, b):
    return lax.dot_general(a, b, (((1,), (1,)), ((), ())), preferred_element_type=F32)


def split(value):
    high = value.astype(BF16)
    return high, (value - high.astype(F32)).astype(BF16)


def fused(
    n, heads, reach, tok, wq, wk, wv, wo, dirs, taps, part_out, att_in, o_w_in, kmix,
    x, q_w, k_w, v_w, o_w, dirs_v, taps_v, taps_pad, band, dirs_hi, dirs_lo, norm_w,
    keys, conv, vt, queries, qf, part, part_b, inner_in, outer_b, outer_in, full, gate, att,
    loc, send, recv, inner_send, inner_recv, outer_send, outer_recv, full_send, full_recv,
):
    rows, half = tok.shape
    features = dirs.shape[1]
    out_cols = part_out.shape[1]
    width = heads * HEAD_DIM
    pairs = width // LANES
    group, block = heads, 2 * reach
    outer = n // group
    cuts = (pl.ds(0, HEAD_DIM // 2), pl.ds(HEAD_DIM // 2, HEAD_DIM // 2 + PAD))
    scale = HEAD_DIM ** (-0.25)
    me, core = lax.axis_index("seq"), lax.axis_index("head")
    other = 1 - core
    spot, plane = lax.rem(me, group), lax.div(me, group)

    def inner_spot(d):
        found, weight = 0, 1
        while weight < group:
            bit = lax.rem(lax.div(spot, weight), 2)
            found = found + weight * (1 - bit if d & weight else bit)
            weight *= 2
        return found

    def inner_peer(d):
        return plane * group + inner_spot(d)

    def other_plane(k):
        return k + (plane <= k).astype(jnp.int32)

    low_side = (2 * plane < outer).astype(jnp.int32)

    def far_plane(k):
        top = outer - 1 - k
        return low_side * (top - (plane >= top).astype(jnp.int32)) + (1 - low_side) * other_plane(k)

    def outer_peer(k):
        return far_plane(k) * group + spot

    barrier = pltpu.get_barrier_semaphore()

    def greet(seq_id, core_id):
        pl.semaphore_signal(barrier, inc=1, device_id=(seq_id, core_id), device_id_type=MESH)

    for k in range(outer - 1):
        greet(outer_peer(k), core)

    @pl.when(me > 0)
    def _():
        greet(me - 1, core)

    @pl.when(me < n - 1)
    def _():
        greet(me + 1, core)

    for d in range(1, group):
        greet(inner_peer(d), core)
    greet(me, other)

    own_cols = pl.ds(pl.multiple_of(core * half, LANES), half)
    main = pl.ds(reach, rows)
    my_out = pl.ds(pl.multiple_of(core * out_cols, LANES), out_cols)
    other_out = pl.ds(pl.multiple_of(other * out_cols, LANES), out_cols)
    local = [
        pltpu.make_async_copy(src, dst, loc.at[at])
        for at, (src, dst) in enumerate(
            [
                (tok, x.at[main, own_cols]),
                (wk, k_w),
                (wv, v_w),
                (dirs, dirs_v),
                (taps, taps_v),
                (wq, q_w),
                (wo.at[:, my_out], o_w),
            ]
        )
    ]
    for copy in local:
        copy.start()

    @pl.when(me == 0)
    def _():
        x[0:reach, :] = jnp.zeros((reach, x.shape[1]), BF16)

    @pl.when(me == n - 1)
    def _():
        x[reach + rows :, :] = jnp.zeros((reach, x.shape[1]), BF16)

    sides = ((me > 0).astype(jnp.int32) + (me < n - 1).astype(jnp.int32))
    pl.semaphore_wait(barrier, outer - 1 + group + sides)

    def remote(src, dst, at, seq_id, core_id):
        return pltpu.make_async_remote_copy(
            src_ref=src, dst_ref=dst, send_sem=send.at[at], recv_sem=recv.at[at],
            device_id=(seq_id, core_id), device_id_type=MESH,
        )

    swap_tok = remote(tok, x.at[main, own_cols], 0, me, other)
    pieces = 2
    part_rows = reach // pieces
    lower, upper, lower_on, upper_on = [], [], [], []
    for k in range(pieces):
        low = x.at[pl.ds(reach + rows + k * part_rows, part_rows), own_cols]
        high = x.at[pl.ds(k * part_rows, part_rows), own_cols]
        lower.append(remote(tok.at[pl.ds(k * part_rows, part_rows), :], low, 4 + k, me - 1, core))
        upper.append(
            remote(tok.at[pl.ds(rows - reach + k * part_rows, part_rows), :], high, 6 + k, me + 1, core)
        )
        lower_on.append(remote(low, low, 8 + k, me, other))
        upper_on.append(remote(high, high, 10 + k, me, other))
    swap_out = remote(wo.at[:, other_out], o_w_in, 1, me, other)

    @pl.when(me > 0)
    def _():
        for copy in lower:
            copy.start()

    @pl.when(me < n - 1)
    def _():
        for copy in upper:
            copy.start()

    swap_tok.start()

    dirs_hi[...] = jnp.zeros(dirs_hi.shape, BF16)
    dirs_lo[...] = jnp.zeros(dirs_lo.shape, BF16)
    norm_w[...] = jnp.zeros(norm_w.shape, BF16)
    gate[...] = jnp.zeros(gate.shape, BF16)
    taps_pad[...] = jnp.zeros(taps_pad.shape, F32)
    for h in range(heads):
        r, c = slice(h * HEAD_DIM, (h + 1) * HEAD_DIM), slice(h * features, (h + 1) * features)
        norm_w[r, c] = jnp.full((HEAD_DIM, features), 0.5 * HEAD_DIM ** (-0.5), BF16)
        vt[h, HEAD_DIM:, :] = jnp.ones((PAD, rows), BF16)
    local[3].wait()
    dir_high, dir_low = split(dirs_v[...] * scale)
    for h in range(heads):
        r, c = slice(h * HEAD_DIM, (h + 1) * HEAD_DIM), slice(h * features, (h + 1) * features)
        dirs_hi[r, c] = dir_high
        dirs_lo[r, c] = dir_low
    local[4].wait()
    taps_pad[0:heads, 0 : block + 1] = taps_v[...].astype(F32)
    for h in range(heads):
        row = jnp.broadcast_to(taps_pad[h : h + 1, :], (block, 2 * block))
        band[h * block : (h + 1) * block, :] = pltpu.roll(row, 0, 1, stride=1, stride_axis=0).astype(BF16)

    local[0].wait()
    local[1].wait()
    swap_tok.wait_recv()
    keys[reach : reach + rows, :] = mm(x[reach : reach + rows, :], k_w[...]).astype(BF16)
    local[2].wait()
    values_t = mm(x[reach : reach + rows, :], v_w[...]).T.astype(BF16)
    for h in range(heads):
        vt[h, 0:HEAD_DIM, :] = values_t[h * HEAD_DIM : (h + 1) * HEAD_DIM, :]

    @pl.when(me > 0)
    def _():
        for copy, on in zip(upper, upper_on):
            copy.wait_recv()
            on.start()

    @pl.when(me < n - 1)
    def _():
        for copy, on in zip(lower, lower_on):
            copy.wait_recv()
            on.start()

    @pl.when(me > 0)
    def _():
        for on in upper_on:
            on.wait_recv()

    @pl.when(me < n - 1)
    def _():
        for on in lower_on:
            on.wait_recv()

    keys[0:reach, :] = mm(x[0:reach, :], k_w[...]).astype(BF16)
    keys[reach + rows :, :] = mm(x[reach + rows :, :], k_w[...]).astype(BF16)

    lane = lax.broadcasted_iota(jnp.int32, (block, LANES), 1)
    for b in range(rows // block):
        for p in range(pairs):
            got = mm(
                band[2 * p * block : 2 * (p + 1) * block, :],
                keys[b * block : (b + 2) * block, p * LANES : (p + 1) * LANES],
            )
            conv[b * block : (b + 1) * block, p * LANES : (p + 1) * LANES] = jnp.where(
                lane < HEAD_DIM, got[:block], got[block:]
            )
    c = conv[...]
    c_hi, c_lo = split(c)
    kmix[...] = c_hi
    sq_hi, sq_lo = split(c * c)
    logits = mm(c_hi, dirs_hi[...]) + mm(c_lo, dirs_hi[...]) + mm(c_hi, dirs_lo[...])
    logits = logits - (mm(sq_hi, norm_w[...]) + mm(sq_lo, norm_w[...]))
    kf = jnp.exp(logits).astype(BF16)
    for h in range(heads):
        got = mm(vt[h], kf[:, h * features : (h + 1) * features])
        part[h] = got
        part_b[h] = got.astype(BF16)

    order = range(group - 1, 0, -1)
    scatter = [
        [
            pltpu.make_async_remote_copy(
                src_ref=part_b.at[inner_spot(d), at, :], dst_ref=inner_in.at[d - 1, at, :],
                send_sem=inner_send.at[t, d - 1], recv_sem=inner_recv.at[t, d - 1],
                device_id=(inner_peer(d), core), device_id_type=MESH,
            )
            for d in order
        ]
        for t, at in enumerate(cuts)
    ]
    for copy in scatter[0] + scatter[1]:
        copy.start()
    swap_out.start()
    local[5].wait()
    queries[...] = mm(x[reach : reach + rows, :], q_w[...]).astype(BF16)
    spread, sums = [], []
    for t, at in enumerate(cuts):
        mine = part[spot, at, :]
        for copy, d in zip(scatter[t], order):
            copy.wait_recv()
            mine = mine + inner_in[d - 1, at, :].astype(F32)
        outer_b[at, :] = mine.astype(BF16)
        sums.append(mine)
        for k in range(outer - 1):
            copy = pltpu.make_async_remote_copy(
                src_ref=outer_b.at[at, :], dst_ref=outer_in.at[plane, at, :],
                send_sem=outer_send.at[t, k], recv_sem=outer_recv.at[t, plane],
                device_id=(outer_peer(k), core), device_id_type=MESH,
            )
            copy.start()
            spread.append(copy)
    q = queries[...]
    qf[...] = jnp.exp(mm(q, dirs_hi[...]) + mm(q, dirs_lo[...])).astype(BF16)
    gather = []
    for t, at in enumerate(cuts):
        mine = sums[t]
        for k in range(outer - 1):
            source = other_plane(k)
            pltpu.make_async_remote_copy(
                src_ref=outer_b.at[at, :], dst_ref=outer_in.at[source, at, :],
                send_sem=outer_send.at[t, k], recv_sem=outer_recv.at[t, source],
                device_id=(outer_peer(k), core), device_id_type=MESH,
            ).wait_recv()
            mine = mine + outer_in[source, at, :].astype(F32)
        full[spot, at, :] = mine.astype(BF16)
        for d in order:
            copy = pltpu.make_async_remote_copy(
                src_ref=full.at[spot, at, :], dst_ref=full.at[spot, at, :],
                send_sem=full_send.at[t, d - 1], recv_sem=full_recv.at[t, d - 1],
                device_id=(inner_peer(d), core), device_id_type=MESH,
            )
            copy.start()
            gather.append(copy)
    for copy in gather:
        copy.wait_recv()

    for h in range(heads):
        p, k = divmod(h, 2)
        r = slice(k * HEAD_DIM, (k + 1) * HEAD_DIM)
        s = slice(LANES + k * HEAD_DIM, LANES + (k + 1) * HEAD_DIM)
        f = slice(k * features, (k + 1) * features)
        gate[p, r, f] = full[h, 0:HEAD_DIM, :]
        gate[p, s, f] = jnp.broadcast_to(full[h, HEAD_DIM : HEAD_DIM + 1, :], (HEAD_DIM, features))
    steps = 2
    span = rows // steps
    swap_att = []
    for b in range(steps):
        r = slice(b * span, (b + 1) * span)
        for p in range(pairs):
            got = mm_nt(qf[r, 2 * p * features : 2 * (p + 1) * features], gate[p])
            att[r, p * LANES : (p + 1) * LANES] = (got[:, :LANES] / got[:, LANES:]).astype(BF16)
        piece = pl.ds(b * span, span)
        copy = remote(att.at[piece, :], att_in.at[piece, :], 2 + b, me, other)
        copy.start()
        swap_att.append(copy)
    local[6].wait()
    part_out[...] = mm(att[...], o_w[...])
    swap_out.wait_recv()
    for copy in swap_att:
        copy.wait_recv()
    for copy in [swap_tok, swap_out] + scatter[0] + scatter[1] + spread + gather + swap_att:
        copy.wait_send()

    @pl.when(me > 0)
    def _():
        for copy in lower + upper_on:
            copy.wait_send()

    @pl.when(me < n - 1)
    def _():
        for copy in upper + lower_on:
            copy.wait_send()


def finish(part_in, att_in, o_w_in, kmix, mixed, key_mixed, out_v, sem):
    rows = att_in.shape[0]
    out_keys = pltpu.make_async_copy(kmix, key_mixed, sem.at[0])
    out_keys.start()
    outs = []
    steps = 2
    span = rows // steps
    for b in range(steps):
        r = slice(b * span, (b + 1) * span)
        out_v[r, :] = (part_in[r, :] + mm(att_in[r, :], o_w_in[...])).astype(BF16)
        piece = pl.ds(b * span, span)
        outs.append(pltpu.make_async_copy(out_v.at[piece, :], mixed.at[piece, :], sem.at[1 + b]))
        outs[b].start()
    out_keys.wait()
    for copy in outs:
        copy.wait()


def body(n, tokens, w_query, w_key, w_value, w_out, feature_dirs, kernel_taps):
    rows, half = tokens.shape
    d = w_key.shape[0]
    width = w_key.shape[1]
    heads = width // HEAD_DIM
    features = feature_dirs.shape[1]
    reach = (kernel_taps.shape[1] - 1) // 2
    block = 2 * reach
    out_cols = w_out.shape[1] // 2
    outer = n // heads
    chunk = HEAD_DIM + PAD
    vmem = pltpu.VMEM
    dma = pltpu.SemaphoreType.DMA
    any_spec = pl.BlockSpec(memory_space=pl.ANY)
    vmem_spec = pl.BlockSpec(memory_space=pltpu.VMEM)
    held = pl.pallas_call(
        functools.partial(fused, n, heads, reach),
        out_shape=(
            vmem((rows, out_cols), F32),
            vmem((rows, width), BF16),
            vmem((width, out_cols), BF16),
            vmem((rows, width), BF16),
        ),
        in_specs=[any_spec] * 7,
        out_specs=(vmem_spec,) * 4,
        scratch_shapes=[
            vmem((rows + 2 * reach, d), BF16),
            vmem((d, width), BF16),
            vmem((d, width), BF16),
            vmem((d, width), BF16),
            vmem((width, out_cols), BF16),
            vmem(feature_dirs.shape, F32),
            vmem(kernel_taps.shape, BF16),
            vmem((8, 2 * block), F32),
            vmem((heads * block, 2 * block), BF16),
            vmem((width, heads * features), BF16),
            vmem((width, heads * features), BF16),
            vmem((width, heads * features), BF16),
            vmem((rows + 2 * reach, width), BF16),
            vmem((rows, width), F32),
            vmem((heads, chunk, rows), BF16),
            vmem((rows, width), BF16),
            vmem((rows, heads * features), BF16),
            vmem((heads, chunk, features), F32),
            vmem((heads, chunk, features), BF16),
            vmem((heads - 1, chunk, features), BF16),
            vmem((chunk, features), BF16),
            vmem((outer, chunk, features), BF16),
            vmem((heads, chunk, features), BF16),
            vmem((width // LANES, 2 * LANES, 2 * features), BF16),
            vmem((rows, width), BF16),
            dma((7,)),
            dma((12,)),
            dma((12,)),
            dma((2, heads - 1)),
            dma((2, heads - 1)),
            dma((2, max(outer - 1, 1))),
            dma((2, outer)),
            dma((2, heads - 1)),
            dma((2, heads - 1)),
        ],
        compiler_params=pltpu.CompilerParams(collective_id=0, has_side_effects=True),
        name="fused",
    )(tokens, w_query, w_key, w_value, w_out, feature_dirs, kernel_taps)
    return pl.pallas_call(
        finish,
        out_shape=(
            jax.ShapeDtypeStruct((rows, out_cols), BF16),
            jax.ShapeDtypeStruct((rows, width), BF16),
        ),
        in_specs=[vmem_spec] * 4,
        out_specs=(any_spec, any_spec),
        scratch_shapes=[vmem((rows, out_cols), BF16), dma((3,))],
        name="finish",
    )(*[pltpu.with_memory_space_constraint(a, pltpu.VMEM) for a in held])


def solution(mesh):
    return jax.shard_map(
        functools.partial(body, mesh.shape["seq"]),
        mesh=mesh,
        in_specs=(
            P("seq", "head"),
            P(None, "head"),
            P(None, "head"),
            P(None, "head"),
            P("head", None),
            P(),
            P("head", None),
        ),
        out_specs=(P("seq", "head"), P("seq", "head")),
        check_vma=False,
    )
```

```python
import functools

import jax
import jax.numpy as jnp
from jax import lax
from jax.experimental import pallas as pl
from jax.experimental.pallas import tpu as pltpu
from jax.sharding import PartitionSpec as P

HEAD_DIM = 64
LANES = 128
PAD = 8
MESH = pl.DeviceIdType.MESH
F32, BF16 = jnp.float32, jnp.bfloat16


def mm(a, b):
    return jnp.dot(a, b, preferred_element_type=F32)


def mm_nt(a, b):
    return lax.dot_general(a, b, (((1,), (1,)), ((), ())), preferred_element_type=F32)


def split(value):
    high = value.astype(BF16)
    return high, (value - high.astype(F32)).astype(BF16)


def fused(
    n, heads, reach, tok, wq, wk, wv, wo, dirs, taps, part_out, att_in, o_w_in, kmix,
    x, q_w, k_w, v_w, o_w, dirs_v, taps_v, taps_pad, band, dirs_hi, dirs_lo, norm_w,
    keys, vt, queries, qf, part, part_b, inner_in, outer_b, outer_in, full, gate, att,
    loc, send, recv, inner_send, inner_recv, outer_send, outer_recv, full_send, full_recv,
):
    rows, half = tok.shape
    features = dirs.shape[1]
    out_cols = part_out.shape[1]
    width = heads * HEAD_DIM
    pairs = width // LANES
    group, block = heads, 2 * reach
    outer = n // group
    cuts = (pl.ds(0, HEAD_DIM + PAD),)
    scale = HEAD_DIM ** (-0.25)
    me, core = lax.axis_index("seq"), lax.axis_index("head")
    other = 1 - core
    spot, plane = lax.rem(me, group), lax.div(me, group)

    def inner_spot(d):
        found, weight = 0, 1
        while weight < group:
            bit = lax.rem(lax.div(spot, weight), 2)
            found = found + weight * (1 - bit if d & weight else bit)
            weight *= 2
        return found

    def inner_peer(d):
        return plane * group + inner_spot(d)

    def other_plane(k):
        return k + (plane <= k).astype(jnp.int32)

    low_side = (2 * plane < outer).astype(jnp.int32)

    def far_plane(k):
        top = outer - 1 - k
        return low_side * (top - (plane >= top).astype(jnp.int32)) + (1 - low_side) * other_plane(k)

    def outer_peer(k):
        return far_plane(k) * group + spot

    barrier = pltpu.get_barrier_semaphore()

    def greet(seq_id, core_id):
        pl.semaphore_signal(barrier, inc=1, device_id=(seq_id, core_id), device_id_type=MESH)

    for k in range(outer - 1):
        greet(outer_peer(k), core)

    @pl.when(me > 0)
    def _():
        greet(me - 1, core)

    @pl.when(me < n - 1)
    def _():
        greet(me + 1, core)

    for d in range(1, group):
        greet(inner_peer(d), core)
    greet(me, other)

    own_cols = pl.ds(pl.multiple_of(core * half, LANES), half)
    main = pl.ds(reach, rows)
    my_out = pl.ds(pl.multiple_of(core * out_cols, LANES), out_cols)
    other_out = pl.ds(pl.multiple_of(other * out_cols, LANES), out_cols)
    local = [
        pltpu.make_async_copy(src, dst, loc.at[at])
        for at, (src, dst) in enumerate(
            [
                (tok, x.at[main, own_cols]),
                (wk, k_w),
                (wv, v_w),
                (dirs, dirs_v),
                (taps, taps_v),
                (wq, q_w),
                (wo.at[:, my_out], o_w),
            ]
        )
    ]
    for copy in local:
        copy.start()

    @pl.when(me == 0)
    def _():
        x[0:reach, :] = jnp.zeros((reach, x.shape[1]), BF16)

    @pl.when(me == n - 1)
    def _():
        x[reach + rows :, :] = jnp.zeros((reach, x.shape[1]), BF16)

    sides = ((me > 0).astype(jnp.int32) + (me < n - 1).astype(jnp.int32))
    pl.semaphore_wait(barrier, outer - 1 + group + sides)

    def remote(src, dst, at, seq_id, core_id):
        return pltpu.make_async_remote_copy(
            src_ref=src, dst_ref=dst, send_sem=send.at[at], recv_sem=recv.at[at],
            device_id=(seq_id, core_id), device_id_type=MESH,
        )

    swap_tok = remote(tok, x.at[main, own_cols], 0, me, other)
    pieces = 2
    part_rows = reach // pieces
    lower, upper, lower_on, upper_on = [], [], [], []
    for k in range(pieces):
        low = x.at[pl.ds(reach + rows + k * part_rows, part_rows), own_cols]
        high = x.at[pl.ds(k * part_rows, part_rows), own_cols]
        lower.append(remote(tok.at[pl.ds(k * part_rows, part_rows), :], low, 4 + k, me - 1, core))
        upper.append(
            remote(tok.at[pl.ds(rows - reach + k * part_rows, part_rows), :], high, 6 + k, me + 1, core)
        )
        lower_on.append(remote(low, low, 8 + k, me, other))
        upper_on.append(remote(high, high, 10 + k, me, other))
    swap_out = remote(wo.at[:, other_out], o_w_in, 1, me, other)

    @pl.when(me > 0)
    def _():
        for copy in lower:
            copy.start()

    @pl.when(me < n - 1)
    def _():
        for copy in upper:
            copy.start()

    swap_tok.start()

    dirs_hi[...] = jnp.zeros(dirs_hi.shape, BF16)
    dirs_lo[...] = jnp.zeros(dirs_lo.shape, BF16)
    norm_w[...] = jnp.zeros(norm_w.shape, BF16)
    gate[...] = jnp.zeros(gate.shape, BF16)
    taps_pad[...] = jnp.zeros(taps_pad.shape, F32)
    for h in range(heads):
        r, c = slice(h * HEAD_DIM, (h + 1) * HEAD_DIM), slice(h * features, (h + 1) * features)
        norm_w[r, c] = jnp.full((HEAD_DIM, features), 0.5 * HEAD_DIM ** (-0.5), BF16)
        vt[h, HEAD_DIM:, :] = jnp.ones((PAD, rows), BF16)
    local[3].wait()
    dir_high, dir_low = split(dirs_v[...] * scale)
    for h in range(heads):
        r, c = slice(h * HEAD_DIM, (h + 1) * HEAD_DIM), slice(h * features, (h + 1) * features)
        dirs_hi[r, c] = dir_high
        dirs_lo[r, c] = dir_low
    local[4].wait()
    taps_pad[0:heads, 0 : block + 1] = taps_v[...].astype(F32)
    for h in range(heads):
        row = jnp.broadcast_to(taps_pad[h : h + 1, :], (block, 2 * block))
        band[h * block : (h + 1) * block, :] = pltpu.roll(row, 0, 1, stride=1, stride_axis=0).astype(BF16)

    local[0].wait()
    local[1].wait()
    swap_tok.wait_recv()
    keys[reach : reach + rows, :] = mm(x[reach : reach + rows, :], k_w[...]).astype(BF16)
    local[2].wait()
    values = mm(x[reach : reach + rows, :], v_w[...])
    values_t = jnp.concatenate([values[reach : rows - reach], values[:reach], values[rows - reach :]], axis=0).T
    values_t = values_t.astype(BF16)
    for h in range(heads):
        vt[h, 0:HEAD_DIM, :] = values_t[h * HEAD_DIM : (h + 1) * HEAD_DIM, :]

    lane = lax.broadcasted_iota(jnp.int32, (block, LANES), 1)

    def key_feats(c):
        c_hi, c_lo = split(c)
        sq_hi, sq_lo = split(c * c)
        logits = mm(c_hi, dirs_hi[...]) + mm(c_lo, dirs_hi[...]) + mm(c_hi, dirs_lo[...])
        logits = logits - (mm(sq_hi, norm_w[...]) + mm(sq_lo, norm_w[...]))
        return c_hi, jnp.exp(logits).astype(BF16)

    inside = rows - block
    for b in range(inside // block):
        sides_of = []
        for p in range(pairs):
            got = mm(
                band[2 * p * block : 2 * (p + 1) * block, :],
                keys[reach + b * block : reach + (b + 2) * block, p * LANES : (p + 1) * LANES],
            )
            sides_of.append(jnp.where(lane < HEAD_DIM, got[:block], got[block:]))
        mix, kf = key_feats(jnp.concatenate(sides_of, axis=1))
        kmix[reach + b * block : reach + (b + 1) * block, :] = mix
        for h in range(heads):
            got = mm(vt[h, :, b * block : (b + 1) * block], kf[:, h * features : (h + 1) * features])
            part[h] = got if b == 0 else part[h] + got

    @pl.when(me > 0)
    def _():
        for copy, on in zip(upper, upper_on):
            copy.wait_recv()
            on.start()

    @pl.when(me < n - 1)
    def _():
        for copy, on in zip(lower, lower_on):
            copy.wait_recv()
            on.start()

    @pl.when(me > 0)
    def _():
        for on in upper_on:
            on.wait_recv()

    @pl.when(me < n - 1)
    def _():
        for on in lower_on:
            on.wait_recv()

    ends = mm(jnp.concatenate([x[0:reach, :], x[reach + rows :, :]], axis=0), k_w[...]).astype(BF16)
    span3 = 3 * reach
    low_keys = jnp.concatenate([ends[:reach], keys[reach:span3, :]], axis=0)
    high_keys = jnp.concatenate([keys[rows - reach : rows + reach, :], ends[reach:]], axis=0)
    edge = lane[:reach] < HEAD_DIM
    lows, highs = [], []
    for p in range(pairs):
        r, cols = 2 * p * block, slice(p * LANES, (p + 1) * LANES)
        taps_two = jnp.concatenate(
            [band[r : r + reach, :span3], band[r + block : r + block + reach, :span3]], axis=0
        )
        got = mm(taps_two, jnp.concatenate([low_keys[:, cols], high_keys[:, cols]], axis=1))
        lows.append(jnp.where(edge, got[:reach, :LANES], got[reach:, :LANES]))
        highs.append(jnp.where(edge, got[:reach, LANES:], got[reach:, LANES:]))
    mix, kf = key_feats(
        jnp.concatenate([jnp.concatenate(lows, axis=1), jnp.concatenate(highs, axis=1)], axis=0)
    )
    kmix[0:reach, :] = mix[:reach]
    kmix[rows - reach :, :] = mix[reach:]
    for h in range(heads):
        got = mm(vt[h, :, inside:], kf[:, h * features : (h + 1) * features])
        got = part[h] + got if inside else got
        part[h] = got
        part_b[h] = got.astype(BF16)

    order = range(group - 1, 0, -1)
    scatter = [
        [
            pltpu.make_async_remote_copy(
                src_ref=part_b.at[inner_spot(d), at, :], dst_ref=inner_in.at[d - 1, at, :],
                send_sem=inner_send.at[t, d - 1], recv_sem=inner_recv.at[t, d - 1],
                device_id=(inner_peer(d), core), device_id_type=MESH,
            )
            for d in order
        ]
        for t, at in enumerate(cuts)
    ]
    for copy in sum(scatter, []):
        copy.start()
    swap_out.start()
    local[5].wait()
    queries[...] = mm(x[reach : reach + rows, :], q_w[...]).astype(BF16)
    spread, sums = [], []
    for t, at in enumerate(cuts):
        mine = part[spot, at, :]
        for copy, d in zip(scatter[t], order):
            copy.wait_recv()
            mine = mine + inner_in[d - 1, at, :].astype(F32)
        outer_b[at, :] = mine.astype(BF16)
        sums.append(mine)
        for k in range(outer - 1):
            copy = pltpu.make_async_remote_copy(
                src_ref=outer_b.at[at, :], dst_ref=outer_in.at[plane, at, :],
                send_sem=outer_send.at[t, k], recv_sem=outer_recv.at[t, plane],
                device_id=(outer_peer(k), core), device_id_type=MESH,
            )
            copy.start()
            spread.append(copy)
    q = queries[...]
    qf[...] = jnp.exp(mm(q, dirs_hi[...]) + mm(q, dirs_lo[...])).astype(BF16)
    gather = []
    for t, at in enumerate(cuts):
        mine = sums[t]
        for k in range(outer - 1):
            source = other_plane(k)
            pltpu.make_async_remote_copy(
                src_ref=outer_b.at[at, :], dst_ref=outer_in.at[source, at, :],
                send_sem=outer_send.at[t, k], recv_sem=outer_recv.at[t, source],
                device_id=(outer_peer(k), core), device_id_type=MESH,
            ).wait_recv()
            mine = mine + outer_in[source, at, :].astype(F32)
        full[spot, at, :] = mine.astype(BF16)
        for d in order:
            copy = pltpu.make_async_remote_copy(
                src_ref=full.at[spot, at, :], dst_ref=full.at[spot, at, :],
                send_sem=full_send.at[t, d - 1], recv_sem=full_recv.at[t, d - 1],
                device_id=(inner_peer(d), core), device_id_type=MESH,
            )
            copy.start()
            gather.append(copy)
    for copy in gather:
        copy.wait_recv()

    for h in range(heads):
        p, k = divmod(h, 2)
        r = slice(k * HEAD_DIM, (k + 1) * HEAD_DIM)
        s = slice(LANES + k * HEAD_DIM, LANES + (k + 1) * HEAD_DIM)
        f = slice(k * features, (k + 1) * features)
        gate[p, r, f] = full[h, 0:HEAD_DIM, :]
        gate[p, s, f] = jnp.broadcast_to(full[h, HEAD_DIM : HEAD_DIM + 1, :], (HEAD_DIM, features))
    steps = 2
    span = rows // steps
    swap_att = []
    for b in range(steps):
        r = slice(b * span, (b + 1) * span)
        for p in range(pairs):
            got = mm_nt(qf[r, 2 * p * features : 2 * (p + 1) * features], gate[p])
            att[r, p * LANES : (p + 1) * LANES] = (got[:, :LANES] / got[:, LANES:]).astype(BF16)
        piece = pl.ds(b * span, span)
        copy = remote(att.at[piece, :], att_in.at[piece, :], 2 + b, me, other)
        copy.start()
        swap_att.append(copy)
    local[6].wait()
    part_out[...] = mm(att[...], o_w[...])
    swap_out.wait_recv()
    for copy in swap_att:
        copy.wait_recv()
    for copy in [swap_tok, swap_out] + sum(scatter, []) + spread + gather + swap_att:
        copy.wait_send()

    @pl.when(me > 0)
    def _():
        for copy in lower + upper_on:
            copy.wait_send()

    @pl.when(me < n - 1)
    def _():
        for copy in upper + lower_on:
            copy.wait_send()


def finish(part_in, att_in, o_w_in, kmix, mixed, key_mixed, out_v, sem):
    rows = att_in.shape[0]
    out_keys = pltpu.make_async_copy(kmix, key_mixed, sem.at[0])
    out_keys.start()
    outs = []
    steps = 2
    span = rows // steps
    for b in range(steps):
        r = slice(b * span, (b + 1) * span)
        out_v[r, :] = (part_in[r, :] + mm(att_in[r, :], o_w_in[...])).astype(BF16)
        piece = pl.ds(b * span, span)
        outs.append(pltpu.make_async_copy(out_v.at[piece, :], mixed.at[piece, :], sem.at[1 + b]))
        outs[b].start()
    out_keys.wait()
    for copy in outs:
        copy.wait()


def body(n, tokens, w_query, w_key, w_value, w_out, feature_dirs, kernel_taps):
    rows, half = tokens.shape
    d = w_key.shape[0]
    width = w_key.shape[1]
    heads = width // HEAD_DIM
    features = feature_dirs.shape[1]
    reach = (kernel_taps.shape[1] - 1) // 2
    block = 2 * reach
    out_cols = w_out.shape[1] // 2
    outer = n // heads
    chunk = HEAD_DIM + PAD
    vmem = pltpu.VMEM
    dma = pltpu.SemaphoreType.DMA
    any_spec = pl.BlockSpec(memory_space=pl.ANY)
    vmem_spec = pl.BlockSpec(memory_space=pltpu.VMEM)
    held = pl.pallas_call(
        functools.partial(fused, n, heads, reach),
        out_shape=(
            vmem((rows, out_cols), F32),
            vmem((rows, width), BF16),
            vmem((width, out_cols), BF16),
            vmem((rows, width), BF16),
        ),
        in_specs=[any_spec] * 7,
        out_specs=(vmem_spec,) * 4,
        scratch_shapes=[
            vmem((rows + 2 * reach, d), BF16),
            vmem((d, width), BF16),
            vmem((d, width), BF16),
            vmem((d, width), BF16),
            vmem((width, out_cols), BF16),
            vmem(feature_dirs.shape, F32),
            vmem(kernel_taps.shape, BF16),
            vmem((8, 2 * block), F32),
            vmem((heads * block, 2 * block), BF16),
            vmem((width, heads * features), BF16),
            vmem((width, heads * features), BF16),
            vmem((width, heads * features), BF16),
            vmem((rows + 2 * reach, width), BF16),
            vmem((heads, chunk, rows), BF16),
            vmem((rows, width), BF16),
            vmem((rows, heads * features), BF16),
            vmem((heads, chunk, features), F32),
            vmem((heads, chunk, features), BF16),
            vmem((heads - 1, chunk, features), BF16),
            vmem((chunk, features), BF16),
            vmem((outer, chunk, features), BF16),
            vmem((heads, chunk, features), BF16),
            vmem((width // LANES, 2 * LANES, 2 * features), BF16),
            vmem((rows, width), BF16),
            dma((7,)),
            dma((12,)),
            dma((12,)),
            dma((1, heads - 1)),
            dma((1, heads - 1)),
            dma((1, max(outer - 1, 1))),
            dma((1, outer)),
            dma((1, heads - 1)),
            dma((1, heads - 1)),
        ],
        compiler_params=pltpu.CompilerParams(collective_id=0, has_side_effects=True),
        name="fused",
    )(tokens, w_query, w_key, w_value, w_out, feature_dirs, kernel_taps)
    return pl.pallas_call(
        finish,
        out_shape=(
            jax.ShapeDtypeStruct((rows, out_cols), BF16),
            jax.ShapeDtypeStruct((rows, width), BF16),
        ),
        in_specs=[vmem_spec] * 4,
        out_specs=(any_spec, any_spec),
        scratch_shapes=[vmem((rows, out_cols), BF16), dma((3,))],
        name="finish",
    )(*[pltpu.with_memory_space_constraint(a, pltpu.VMEM) for a in held])


def solution(mesh):
    return jax.shard_map(
        functools.partial(body, mesh.shape["seq"]),
        mesh=mesh,
        in_specs=(
            P("seq", "head"),
            P(None, "head"),
            P(None, "head"),
            P(None, "head"),
            P("head", None),
            P(),
            P("head", None),
        ),
        out_specs=(P("seq", "head"), P("seq", "head")),
        check_vma=False,
    )
```

```python
import functools

import jax
import jax.numpy as jnp
from jax import lax
from jax.experimental import pallas as pl
from jax.experimental.pallas import tpu as pltpu
from jax.sharding import PartitionSpec as P

HEAD_DIM = 64
LANES = 128
PAD = 8
MESH = pl.DeviceIdType.MESH
F32, BF16 = jnp.float32, jnp.bfloat16


def mm(a, b):
    return jnp.dot(a, b, preferred_element_type=F32)


def mm_nt(a, b):
    return lax.dot_general(a, b, (((1,), (1,)), ((), ())), preferred_element_type=F32)


def split(value):
    high = value.astype(BF16)
    return high, (value - high.astype(F32)).astype(BF16)


def fused(
    n, heads, reach, tok, wq, wk, wv, wo, dirs, taps, qf, qf_in, gate, gate_in, o_w, o_w_in, kmix,
    x, q_w, k_w, v_w, dirs_v, taps_v, taps_pad, band, dirs_hi, dirs_lo, norm_w,
    keys, vt, queries, part, part_b, inner_in, outer_b, outer_in, full, full_in,
    loc, send, recv, inner_send, inner_recv, outer_send, outer_recv, full_send, full_recv,
):
    rows, half = tok.shape
    features = dirs.shape[1]
    out_cols = o_w.shape[1]
    width = heads * HEAD_DIM
    pairs = width // LANES
    group, block = heads, 2 * reach
    outer = n // group
    cuts = (pl.ds(0, HEAD_DIM + PAD),)
    scale = HEAD_DIM ** (-0.25)
    me, core = lax.axis_index("seq"), lax.axis_index("head")
    other = 1 - core
    spot, plane = lax.rem(me, group), lax.div(me, group)

    def inner_spot(d):
        found, weight = 0, 1
        while weight < group:
            bit = lax.rem(lax.div(spot, weight), 2)
            found = found + weight * (1 - bit if d & weight else bit)
            weight *= 2
        return found

    def inner_peer(d):
        return plane * group + inner_spot(d)

    def other_plane(k):
        return k + (plane <= k).astype(jnp.int32)

    low_side = (2 * plane < outer).astype(jnp.int32)

    def far_plane(k):
        top = outer - 1 - k
        return low_side * (top - (plane >= top).astype(jnp.int32)) + (1 - low_side) * other_plane(k)

    def outer_peer(k):
        return far_plane(k) * group + spot

    barrier = pltpu.get_barrier_semaphore()

    def greet(seq_id, core_id):
        pl.semaphore_signal(barrier, inc=1, device_id=(seq_id, core_id), device_id_type=MESH)

    for k in range(outer - 1):
        greet(outer_peer(k), core)

    @pl.when(me > 0)
    def _():
        greet(me - 1, core)

    @pl.when(me < n - 1)
    def _():
        greet(me + 1, core)

    for d in range(1, group):
        greet(inner_peer(d), core)
        greet(inner_peer(d), other)
    greet(me, other)

    own_cols = pl.ds(pl.multiple_of(core * half, LANES), half)
    main = pl.ds(reach, rows)
    my_out = pl.ds(pl.multiple_of(core * out_cols, LANES), out_cols)
    other_out = pl.ds(pl.multiple_of(other * out_cols, LANES), out_cols)
    local = [
        pltpu.make_async_copy(src, dst, loc.at[at])
        for at, (src, dst) in enumerate(
            [
                (tok, x.at[main, own_cols]),
                (wk, k_w),
                (wv, v_w),
                (dirs, dirs_v),
                (taps, taps_v),
                (wq, q_w),
                (wo.at[:, my_out], o_w),
            ]
        )
    ]
    for copy in local:
        copy.start()

    @pl.when(me == 0)
    def _():
        x[0:reach, :] = jnp.zeros((reach, x.shape[1]), BF16)

    @pl.when(me == n - 1)
    def _():
        x[reach + rows :, :] = jnp.zeros((reach, x.shape[1]), BF16)

    sides = ((me > 0).astype(jnp.int32) + (me < n - 1).astype(jnp.int32))
    pl.semaphore_wait(barrier, outer - 1 + 2 * group - 1 + sides)

    def remote(src, dst, at, seq_id, core_id):
        return pltpu.make_async_remote_copy(
            src_ref=src, dst_ref=dst, send_sem=send.at[at], recv_sem=recv.at[at],
            device_id=(seq_id, core_id), device_id_type=MESH,
        )

    swap_tok = remote(tok, x.at[main, own_cols], 0, me, other)
    pieces = 2
    part_rows = reach // pieces
    lower, upper, lower_on, upper_on = [], [], [], []
    for k in range(pieces):
        low = x.at[pl.ds(reach + rows + k * part_rows, part_rows), own_cols]
        high = x.at[pl.ds(k * part_rows, part_rows), own_cols]
        lower.append(remote(tok.at[pl.ds(k * part_rows, part_rows), :], low, 4 + k, me - 1, core))
        upper.append(
            remote(tok.at[pl.ds(rows - reach + k * part_rows, part_rows), :], high, 6 + k, me + 1, core)
        )
        lower_on.append(remote(low, low, 8 + k, me, other))
        upper_on.append(remote(high, high, 10 + k, me, other))
    swap_out = remote(wo.at[:, other_out], o_w_in, 1, me, other)

    @pl.when(me > 0)
    def _():
        for copy in lower:
            copy.start()

    @pl.when(me < n - 1)
    def _():
        for copy in upper:
            copy.start()

    swap_tok.start()

    dirs_hi[...] = jnp.zeros(dirs_hi.shape, BF16)
    dirs_lo[...] = jnp.zeros(dirs_lo.shape, BF16)
    norm_w[...] = jnp.zeros(norm_w.shape, BF16)
    gate[...] = jnp.zeros(gate.shape, BF16)
    gate_in[...] = jnp.zeros(gate_in.shape, BF16)
    taps_pad[...] = jnp.zeros(taps_pad.shape, F32)
    for h in range(heads):
        r, c = slice(h * HEAD_DIM, (h + 1) * HEAD_DIM), slice(h * features, (h + 1) * features)
        norm_w[r, c] = jnp.full((HEAD_DIM, features), 0.5 * HEAD_DIM ** (-0.5), BF16)
        vt[h, HEAD_DIM:, :] = jnp.ones((PAD, rows), BF16)
    local[3].wait()
    dir_high, dir_low = split(dirs_v[...] * scale)
    for h in range(heads):
        r, c = slice(h * HEAD_DIM, (h + 1) * HEAD_DIM), slice(h * features, (h + 1) * features)
        dirs_hi[r, c] = dir_high
        dirs_lo[r, c] = dir_low
    local[4].wait()
    taps_pad[0:heads, 0 : block + 1] = taps_v[...].astype(F32)
    for h in range(heads):
        row = jnp.broadcast_to(taps_pad[h : h + 1, :], (block, 2 * block))
        band[h * block : (h + 1) * block, :] = pltpu.roll(row, 0, 1, stride=1, stride_axis=0).astype(BF16)

    local[0].wait()
    local[1].wait()
    swap_tok.wait_recv()
    keys[reach : reach + rows, :] = mm(x[reach : reach + rows, :], k_w[...]).astype(BF16)
    local[2].wait()
    values = mm(x[reach : reach + rows, :], v_w[...])
    values_t = jnp.concatenate([values[reach : rows - reach], values[:reach], values[rows - reach :]], axis=0).T
    values_t = values_t.astype(BF16)
    for h in range(heads):
        vt[h, 0:HEAD_DIM, :] = values_t[h * HEAD_DIM : (h + 1) * HEAD_DIM, :]

    lane = lax.broadcasted_iota(jnp.int32, (block, LANES), 1)

    def key_feats(c):
        c_hi, c_lo = split(c)
        sq_hi, sq_lo = split(c * c)
        logits = mm(c_hi, dirs_hi[...]) + mm(c_lo, dirs_hi[...]) + mm(c_hi, dirs_lo[...])
        logits = logits - (mm(sq_hi, norm_w[...]) + mm(sq_lo, norm_w[...]))
        return c_hi, jnp.exp(logits).astype(BF16)

    inside = rows - block
    for b in range(inside // block):
        sides_of = []
        for p in range(pairs):
            got = mm(
                band[2 * p * block : 2 * (p + 1) * block, :],
                keys[reach + b * block : reach + (b + 2) * block, p * LANES : (p + 1) * LANES],
            )
            sides_of.append(jnp.where(lane < HEAD_DIM, got[:block], got[block:]))
        mix, kf = key_feats(jnp.concatenate(sides_of, axis=1))
        kmix[reach + b * block : reach + (b + 1) * block, :] = mix
        for h in range(heads):
            got = mm(vt[h, :, b * block : (b + 1) * block], kf[:, h * features : (h + 1) * features])
            part[h] = got if b == 0 else part[h] + got

    @pl.when(me > 0)
    def _():
        for copy, on in zip(upper, upper_on):
            copy.wait_recv()
            on.start()

    @pl.when(me < n - 1)
    def _():
        for copy, on in zip(lower, lower_on):
            copy.wait_recv()
            on.start()

    @pl.when(me > 0)
    def _():
        for on in upper_on:
            on.wait_recv()

    @pl.when(me < n - 1)
    def _():
        for on in lower_on:
            on.wait_recv()

    ends = mm(jnp.concatenate([x[0:reach, :], x[reach + rows :, :]], axis=0), k_w[...]).astype(BF16)
    span3 = 3 * reach
    low_keys = jnp.concatenate([ends[:reach], keys[reach:span3, :]], axis=0)
    high_keys = jnp.concatenate([keys[rows - reach : rows + reach, :], ends[reach:]], axis=0)
    edge = lane[:reach] < HEAD_DIM
    lows, highs = [], []
    for p in range(pairs):
        r, cols = 2 * p * block, slice(p * LANES, (p + 1) * LANES)
        taps_two = jnp.concatenate(
            [band[r : r + reach, :span3], band[r + block : r + block + reach, :span3]], axis=0
        )
        got = mm(taps_two, jnp.concatenate([low_keys[:, cols], high_keys[:, cols]], axis=1))
        lows.append(jnp.where(edge, got[:reach, :LANES], got[reach:, :LANES]))
        highs.append(jnp.where(edge, got[:reach, LANES:], got[reach:, LANES:]))
    mix, kf = key_feats(
        jnp.concatenate([jnp.concatenate(lows, axis=1), jnp.concatenate(highs, axis=1)], axis=0)
    )
    kmix[0:reach, :] = mix[:reach]
    kmix[rows - reach :, :] = mix[reach:]
    for h in range(heads):
        got = mm(vt[h, :, inside:], kf[:, h * features : (h + 1) * features])
        got = part[h] + got if inside else got
        part[h] = got
        part_b[h] = got.astype(BF16)

    order = range(group - 1, 0, -1)
    scatter = [
        [
            pltpu.make_async_remote_copy(
                src_ref=part_b.at[inner_spot(d), at, :], dst_ref=inner_in.at[d - 1, at, :],
                send_sem=inner_send.at[t, d - 1], recv_sem=inner_recv.at[t, d - 1],
                device_id=(inner_peer(d), core), device_id_type=MESH,
            )
            for d in order
        ]
        for t, at in enumerate(cuts)
    ]
    for copy in sum(scatter, []):
        copy.start()
    swap_out.start()
    local[5].wait()
    queries[...] = mm(x[reach : reach + rows, :], q_w[...]).astype(BF16)
    spread, sums = [], []
    for t, at in enumerate(cuts):
        mine = part[spot, at, :]
        for copy, d in zip(scatter[t], order):
            copy.wait_recv()
            mine = mine + inner_in[d - 1, at, :].astype(F32)
        outer_b[at, :] = mine.astype(BF16)
        sums.append(mine)
        for k in range(outer - 1):
            copy = pltpu.make_async_remote_copy(
                src_ref=outer_b.at[at, :], dst_ref=outer_in.at[plane, at, :],
                send_sem=outer_send.at[t, k], recv_sem=outer_recv.at[t, plane],
                device_id=(outer_peer(k), core), device_id_type=MESH,
            )
            copy.start()
            spread.append(copy)
    q = queries[...]
    qf[...] = jnp.exp(mm(q, dirs_hi[...]) + mm(q, dirs_lo[...])).astype(BF16)
    swap_qf = remote(qf, qf_in, 2, me, other)
    swap_qf.start()
    gather = []
    for t, at in enumerate(cuts):
        mine = sums[t]
        for k in range(outer - 1):
            source = other_plane(k)
            pltpu.make_async_remote_copy(
                src_ref=outer_b.at[at, :], dst_ref=outer_in.at[source, at, :],
                send_sem=outer_send.at[t, k], recv_sem=outer_recv.at[t, source],
                device_id=(outer_peer(k), core), device_id_type=MESH,
            ).wait_recv()
            mine = mine + outer_in[source, at, :].astype(F32)
        full[spot, at, :] = mine.astype(BF16)
        targets = [(inner_peer(d), side) for d in order for side in (other, core)] + [(me, other)]
        for k, target in enumerate(targets):
            home = full if k % 2 and k < 2 * group - 2 else full_in
            copy = pltpu.make_async_remote_copy(
                src_ref=full.at[spot, at, :], dst_ref=home.at[spot, at, :],
                send_sem=full_send.at[t, k], recv_sem=full_recv.at[t, k],
                device_id=target, device_id_type=MESH,
            )
            copy.start()
            gather.append(copy)
    local[6].wait()
    swap_out.wait_recv()
    swap_qf.wait_recv()
    for copy in gather:
        copy.wait_recv()
    for home, door in ((full, gate), (full_in, gate_in)):
        for h in range(heads):
            p, k = divmod(h, 2)
            r = slice(k * HEAD_DIM, (k + 1) * HEAD_DIM)
            s = slice(LANES + k * HEAD_DIM, LANES + (k + 1) * HEAD_DIM)
            f = slice(k * features, (k + 1) * features)
            door[p, r, f] = home[h, 0:HEAD_DIM, :]
            door[p, s, f] = jnp.broadcast_to(home[h, HEAD_DIM : HEAD_DIM + 1, :], (HEAD_DIM, features))
    for copy in [swap_tok, swap_out, swap_qf] + sum(scatter, []) + spread + gather:
        copy.wait_send()

    @pl.when(me > 0)
    def _():
        for copy in lower + upper_on:
            copy.wait_send()

    @pl.when(me < n - 1)
    def _():
        for copy in upper + lower_on:
            copy.wait_send()


def finish(qf, qf_in, gate, gate_in, o_w, o_w_in, kmix, mixed, key_mixed, out_v, sem):
    rows = qf.shape[0]
    out_keys = pltpu.make_async_copy(kmix, key_mixed, sem.at[0])
    out_keys.start()
    outs = []
    steps = 2
    span = rows // steps
    pairs, _, deep = gate.shape
    for b in range(steps):
        r = slice(b * span, (b + 1) * span)
        total = None
        for feats, door, w in ((qf, gate, o_w), (qf_in, gate_in, o_w_in)):
            att = []
            for p in range(pairs):
                got = mm_nt(feats[r, p * deep : (p + 1) * deep], door[p])
                att.append((got[:, :LANES] / got[:, LANES:]).astype(BF16))
            got = mm(jnp.concatenate(att, axis=1), w[...])
            total = got if total is None else total + got
        out_v[r, :] = total.astype(BF16)
        piece = pl.ds(b * span, span)
        outs.append(pltpu.make_async_copy(out_v.at[piece, :], mixed.at[piece, :], sem.at[1 + b]))
        outs[b].start()
    out_keys.wait()
    for copy in outs:
        copy.wait()


def body(n, tokens, w_query, w_key, w_value, w_out, feature_dirs, kernel_taps):
    rows, half = tokens.shape
    d = w_key.shape[0]
    width = w_key.shape[1]
    heads = width // HEAD_DIM
    features = feature_dirs.shape[1]
    reach = (kernel_taps.shape[1] - 1) // 2
    block = 2 * reach
    out_cols = w_out.shape[1] // 2
    outer = n // heads
    chunk = HEAD_DIM + PAD
    vmem = pltpu.VMEM
    dma = pltpu.SemaphoreType.DMA
    any_spec = pl.BlockSpec(memory_space=pl.ANY)
    vmem_spec = pl.BlockSpec(memory_space=pltpu.VMEM)
    held = pl.pallas_call(
        functools.partial(fused, n, heads, reach),
        out_shape=(
            vmem((rows, heads * features), BF16),
            vmem((rows, heads * features), BF16),
            vmem((width // LANES, 2 * LANES, 2 * features), BF16),
            vmem((width // LANES, 2 * LANES, 2 * features), BF16),
            vmem((width, out_cols), BF16),
            vmem((width, out_cols), BF16),
            vmem((rows, width), BF16),
        ),
        in_specs=[any_spec] * 7,
        out_specs=(vmem_spec,) * 7,
        scratch_shapes=[
            vmem((rows + 2 * reach, d), BF16),
            vmem((d, width), BF16),
            vmem((d, width), BF16),
            vmem((d, width), BF16),
            vmem(feature_dirs.shape, F32),
            vmem(kernel_taps.shape, BF16),
            vmem((8, 2 * block), F32),
            vmem((heads * block, 2 * block), BF16),
            vmem((width, heads * features), BF16),
            vmem((width, heads * features), BF16),
            vmem((width, heads * features), BF16),
            vmem((rows + 2 * reach, width), BF16),
            vmem((heads, chunk, rows), BF16),
            vmem((rows, width), BF16),
            vmem((heads, chunk, features), F32),
            vmem((heads, chunk, features), BF16),
            vmem((heads - 1, chunk, features), BF16),
            vmem((chunk, features), BF16),
            vmem((outer, chunk, features), BF16),
            vmem((heads, chunk, features), BF16),
            vmem((heads, chunk, features), BF16),
            dma((7,)),
            dma((12,)),
            dma((12,)),
            dma((1, heads - 1)),
            dma((1, heads - 1)),
            dma((1, max(outer - 1, 1))),
            dma((1, outer)),
            dma((1, 2 * heads - 1)),
            dma((1, 2 * heads - 1)),
        ],
        compiler_params=pltpu.CompilerParams(collective_id=0, has_side_effects=True),
        name="fused",
    )(tokens, w_query, w_key, w_value, w_out, feature_dirs, kernel_taps)
    return pl.pallas_call(
        finish,
        out_shape=(
            jax.ShapeDtypeStruct((rows, out_cols), BF16),
            jax.ShapeDtypeStruct((rows, width), BF16),
        ),
        in_specs=[vmem_spec] * 7,
        out_specs=(any_spec, any_spec),
        scratch_shapes=[vmem((rows, out_cols), BF16), dma((3,))],
        name="finish",
    )(*[pltpu.with_memory_space_constraint(a, pltpu.VMEM) for a in held])


def solution(mesh):
    return jax.shard_map(
        functools.partial(body, mesh.shape["seq"]),
        mesh=mesh,
        in_specs=(
            P("seq", "head"),
            P(None, "head"),
            P(None, "head"),
            P(None, "head"),
            P("head", None),
            P(),
            P("head", None),
        ),
        out_specs=(P("seq", "head"), P("seq", "head")),
        check_vma=False,
    )
```

```python
import functools

import jax
import jax.numpy as jnp
from jax import lax
from jax.experimental import pallas as pl
from jax.experimental.pallas import tpu as pltpu
from jax.sharding import PartitionSpec as P

HEAD_DIM = 64
LANES = 128
PAD = 8
MESH = pl.DeviceIdType.MESH
F32, BF16 = jnp.float32, jnp.bfloat16


def mm(a, b):
    return jnp.dot(a, b, preferred_element_type=F32)


def mm_nt(a, b):
    return lax.dot_general(a, b, (((1,), (1,)), ((), ())), preferred_element_type=F32)


def split(value):
    high = value.astype(BF16)
    return high, (value - high.astype(F32)).astype(BF16)


def fused(
    n, heads, reach, tok, wq, wk, wv, wo, dirs, taps, qf, qf_in, gate, gate_in, o_w, o_w_in, kmix,
    x, q_w, k_w, v_w, dirs_v, taps_v, taps_pad, band, dirs_hi, dirs_lo, norm_w,
    keys, vt, queries, part, part_b, inner_in, outer_b, outer_in, full, full_in,
    loc, send, recv, inner_send, inner_recv, outer_send, outer_recv, full_send, full_recv,
):
    rows, half = tok.shape
    features = dirs.shape[1]
    out_cols = o_w.shape[1]
    width = heads * HEAD_DIM
    pairs = width // LANES
    group, block = heads, 2 * reach
    outer = n // group
    cuts = (pl.ds(0, HEAD_DIM + PAD),)
    scale = HEAD_DIM ** (-0.25)
    me, core = lax.axis_index("seq"), lax.axis_index("head")
    other = 1 - core
    spot, plane = lax.rem(me, group), lax.div(me, group)

    def inner_spot(d):
        found, weight = 0, 1
        while weight < group:
            bit = lax.rem(lax.div(spot, weight), 2)
            found = found + weight * (1 - bit if d & weight else bit)
            weight *= 2
        return found

    def inner_peer(d):
        return plane * group + inner_spot(d)

    def other_plane(k):
        return k + (plane <= k).astype(jnp.int32)

    low_side = (2 * plane < outer).astype(jnp.int32)

    def far_plane(k):
        top = outer - 1 - k
        return low_side * (top - (plane >= top).astype(jnp.int32)) + (1 - low_side) * other_plane(k)

    def outer_peer(k):
        return far_plane(k) * group + spot

    barrier = pltpu.get_barrier_semaphore()

    def greet(seq_id, core_id):
        pl.semaphore_signal(barrier, inc=1, device_id=(seq_id, core_id), device_id_type=MESH)

    for k in range(outer - 1):
        greet(outer_peer(k), core)

    @pl.when(me > 0)
    def _():
        greet(me - 1, core)

    @pl.when(me < n - 1)
    def _():
        greet(me + 1, core)

    for d in range(1, group):
        greet(inner_peer(d), core)
        greet(inner_peer(d), other)
    greet(me, other)

    own_cols = pl.ds(pl.multiple_of(core * half, LANES), half)
    main = pl.ds(reach, rows)
    my_out = pl.ds(pl.multiple_of(core * out_cols, LANES), out_cols)
    other_out = pl.ds(pl.multiple_of(other * out_cols, LANES), out_cols)
    local = [
        pltpu.make_async_copy(src, dst, loc.at[at])
        for at, (src, dst) in enumerate(
            [
                (tok, x.at[main, own_cols]),
                (wk, k_w),
                (wv, v_w),
                (dirs, dirs_v),
                (taps, taps_v),
                (wq, q_w),
                (wo.at[:, my_out], o_w),
            ]
        )
    ]
    for copy in local:
        copy.start()

    @pl.when(me == 0)
    def _():
        x[0:reach, :] = jnp.zeros((reach, x.shape[1]), BF16)

    @pl.when(me == n - 1)
    def _():
        x[reach + rows :, :] = jnp.zeros((reach, x.shape[1]), BF16)

    sides = ((me > 0).astype(jnp.int32) + (me < n - 1).astype(jnp.int32))
    pl.semaphore_wait(barrier, outer - 1 + 2 * group - 1 + sides)

    def remote(src, dst, at, seq_id, core_id):
        return pltpu.make_async_remote_copy(
            src_ref=src, dst_ref=dst, send_sem=send.at[at], recv_sem=recv.at[at],
            device_id=(seq_id, core_id), device_id_type=MESH,
        )

    swap_tok = remote(tok, x.at[main, own_cols], 0, me, other)
    pieces = 2
    part_rows = reach // pieces
    lower, upper, lower_on, upper_on = [], [], [], []
    for k in range(pieces):
        low = x.at[pl.ds(reach + rows + k * part_rows, part_rows), own_cols]
        high = x.at[pl.ds(k * part_rows, part_rows), own_cols]
        lower.append(remote(tok.at[pl.ds(k * part_rows, part_rows), :], low, 4 + k, me - 1, core))
        upper.append(
            remote(tok.at[pl.ds(rows - reach + k * part_rows, part_rows), :], high, 6 + k, me + 1, core)
        )
        lower_on.append(remote(low, low, 8 + k, me, other))
        upper_on.append(remote(high, high, 10 + k, me, other))
    swap_out = remote(wo.at[:, other_out], o_w_in, 1, me, other)

    odd = lax.rem(me, 2)

    @pl.when((me < n - 1) & (odd == 1))
    def _():
        for copy in upper:
            copy.start()

    @pl.when(me > 0)
    def _():
        for copy in lower:
            copy.start()

    @pl.when((me < n - 1) & (odd == 0))
    def _():
        for copy in upper:
            copy.start()

    swap_tok.start()

    dirs_hi[...] = jnp.zeros(dirs_hi.shape, BF16)
    dirs_lo[...] = jnp.zeros(dirs_lo.shape, BF16)
    norm_w[...] = jnp.zeros(norm_w.shape, BF16)
    gate[...] = jnp.zeros(gate.shape, BF16)
    gate_in[...] = jnp.zeros(gate_in.shape, BF16)
    taps_pad[...] = jnp.zeros(taps_pad.shape, F32)
    for h in range(heads):
        r, c = slice(h * HEAD_DIM, (h + 1) * HEAD_DIM), slice(h * features, (h + 1) * features)
        norm_w[r, c] = jnp.full((HEAD_DIM, features), 0.5 * HEAD_DIM ** (-0.5), BF16)
        vt[h, HEAD_DIM:, :] = jnp.ones((PAD, rows), BF16)
    local[3].wait()
    dir_high, dir_low = split(dirs_v[...] * scale)
    for h in range(heads):
        r, c = slice(h * HEAD_DIM, (h + 1) * HEAD_DIM), slice(h * features, (h + 1) * features)
        dirs_hi[r, c] = dir_high
        dirs_lo[r, c] = dir_low
    local[4].wait()
    taps_pad[0:heads, 0 : block + 1] = taps_v[...].astype(F32)
    for h in range(heads):
        row = jnp.broadcast_to(taps_pad[h : h + 1, :], (block, 2 * block))
        band[h * block : (h + 1) * block, :] = pltpu.roll(row, 0, 1, stride=1, stride_axis=0).astype(BF16)

    local[0].wait()
    local[1].wait()
    swap_tok.wait_recv()
    keys[reach : reach + rows, :] = mm(x[reach : reach + rows, :], k_w[...]).astype(BF16)
    local[2].wait()
    values = mm(x[reach : reach + rows, :], v_w[...])
    values_t = jnp.concatenate([values[reach : rows - reach], values[:reach], values[rows - reach :]], axis=0).T
    values_t = values_t.astype(BF16)
    for h in range(heads):
        vt[h, 0:HEAD_DIM, :] = values_t[h * HEAD_DIM : (h + 1) * HEAD_DIM, :]

    lane = lax.broadcasted_iota(jnp.int32, (block, LANES), 1)

    def key_feats(c):
        c_hi, c_lo = split(c)
        sq_hi, sq_lo = split(c * c)
        logits = mm(c_hi, dirs_hi[...]) + mm(c_lo, dirs_hi[...]) + mm(c_hi, dirs_lo[...])
        logits = logits - (mm(sq_hi, norm_w[...]) + mm(sq_lo, norm_w[...]))
        return c_hi, jnp.exp(logits).astype(BF16)

    inside = rows - block
    for b in range(inside // block):
        sides_of = []
        for p in range(pairs):
            got = mm(
                band[2 * p * block : 2 * (p + 1) * block, :],
                keys[reach + b * block : reach + (b + 2) * block, p * LANES : (p + 1) * LANES],
            )
            sides_of.append(jnp.where(lane < HEAD_DIM, got[:block], got[block:]))
        mix, kf = key_feats(jnp.concatenate(sides_of, axis=1))
        kmix[reach + b * block : reach + (b + 1) * block, :] = mix
        for h in range(heads):
            got = mm(vt[h, :, b * block : (b + 1) * block], kf[:, h * features : (h + 1) * features])
            part[h] = got if b == 0 else part[h] + got

    @pl.when(me > 0)
    def _():
        for copy, on in zip(upper, upper_on):
            copy.wait_recv()
            on.start()

    @pl.when(me < n - 1)
    def _():
        for copy, on in zip(lower, lower_on):
            copy.wait_recv()
            on.start()

    @pl.when(me > 0)
    def _():
        for on in upper_on:
            on.wait_recv()

    @pl.when(me < n - 1)
    def _():
        for on in lower_on:
            on.wait_recv()

    ends = mm(jnp.concatenate([x[0:reach, :], x[reach + rows :, :]], axis=0), k_w[...]).astype(BF16)
    span3 = 3 * reach
    low_keys = jnp.concatenate([ends[:reach], keys[reach:span3, :]], axis=0)
    high_keys = jnp.concatenate([keys[rows - reach : rows + reach, :], ends[reach:]], axis=0)
    edge = lane[:reach] < HEAD_DIM
    lows, highs = [], []
    for p in range(pairs):
        r, cols = 2 * p * block, slice(p * LANES, (p + 1) * LANES)
        taps_two = jnp.concatenate(
            [band[r : r + reach, :span3], band[r + block : r + block + reach, :span3]], axis=0
        )
        got = mm(taps_two, jnp.concatenate([low_keys[:, cols], high_keys[:, cols]], axis=1))
        lows.append(jnp.where(edge, got[:reach, :LANES], got[reach:, :LANES]))
        highs.append(jnp.where(edge, got[:reach, LANES:], got[reach:, LANES:]))
    mix, kf = key_feats(
        jnp.concatenate([jnp.concatenate(lows, axis=1), jnp.concatenate(highs, axis=1)], axis=0)
    )
    kmix[0:reach, :] = mix[:reach]
    kmix[rows - reach :, :] = mix[reach:]
    for h in range(heads):
        got = mm(vt[h, :, inside:], kf[:, h * features : (h + 1) * features])
        got = part[h] + got if inside else got
        part[h] = got
        part_b[h] = got.astype(BF16)

    order = range(group - 1, 0, -1)
    scatter = [
        [
            pltpu.make_async_remote_copy(
                src_ref=part_b.at[inner_spot(d), at, :], dst_ref=inner_in.at[d - 1, at, :],
                send_sem=inner_send.at[t, d - 1], recv_sem=inner_recv.at[t, d - 1],
                device_id=(inner_peer(d), core), device_id_type=MESH,
            )
            for d in order
        ]
        for t, at in enumerate(cuts)
    ]
    for copy in sum(scatter, []):
        copy.start()
    swap_out.start()
    local[5].wait()
    queries[...] = mm(x[reach : reach + rows, :], q_w[...]).astype(BF16)
    spread, sums = [], []
    for t, at in enumerate(cuts):
        mine = part[spot, at, :]
        for copy, d in zip(scatter[t], order):
            copy.wait_recv()
            mine = mine + inner_in[d - 1, at, :].astype(F32)
        outer_b[at, :] = mine.astype(BF16)
        sums.append(mine)
        for k in range(outer - 1):
            copy = pltpu.make_async_remote_copy(
                src_ref=outer_b.at[at, :], dst_ref=outer_in.at[plane, at, :],
                send_sem=outer_send.at[t, k], recv_sem=outer_recv.at[t, plane],
                device_id=(outer_peer(k), core), device_id_type=MESH,
            )
            copy.start()
            spread.append(copy)
    q = queries[...]
    qf[...] = jnp.exp(mm(q, dirs_hi[...]) + mm(q, dirs_lo[...])).astype(BF16)
    swap_qf = remote(qf, qf_in, 2, me, other)
    swap_qf.start()
    gather = []
    for t, at in enumerate(cuts):
        mine = sums[t]
        for k in range(outer - 1):
            source = other_plane(k)
            pltpu.make_async_remote_copy(
                src_ref=outer_b.at[at, :], dst_ref=outer_in.at[source, at, :],
                send_sem=outer_send.at[t, k], recv_sem=outer_recv.at[t, source],
                device_id=(outer_peer(k), core), device_id_type=MESH,
            ).wait_recv()
            mine = mine + outer_in[source, at, :].astype(F32)
        full[spot, at, :] = mine.astype(BF16)
        targets = [(inner_peer(d), side) for d in order for side in (other, core)] + [(me, other)]
        for k, target in enumerate(targets):
            home = full if k % 2 and k < 2 * group - 2 else full_in
            copy = pltpu.make_async_remote_copy(
                src_ref=full.at[spot, at, :], dst_ref=home.at[spot, at, :],
                send_sem=full_send.at[t, k], recv_sem=full_recv.at[t, k],
                device_id=target, device_id_type=MESH,
            )
            copy.start()
            gather.append(copy)
    local[6].wait()
    swap_out.wait_recv()
    swap_qf.wait_recv()
    for copy in gather:
        copy.wait_recv()
    for home, door in ((full, gate), (full_in, gate_in)):
        for h in range(heads):
            p, k = divmod(h, 2)
            r = slice(k * HEAD_DIM, (k + 1) * HEAD_DIM)
            s = slice(LANES + k * HEAD_DIM, LANES + (k + 1) * HEAD_DIM)
            f = slice(k * features, (k + 1) * features)
            door[p, r, f] = home[h, 0:HEAD_DIM, :]
            door[p, s, f] = jnp.broadcast_to(home[h, HEAD_DIM : HEAD_DIM + 1, :], (HEAD_DIM, features))
    for copy in [swap_tok, swap_out, swap_qf] + sum(scatter, []) + spread + gather:
        copy.wait_send()

    @pl.when(me > 0)
    def _():
        for copy in lower + upper_on:
            copy.wait_send()

    @pl.when(me < n - 1)
    def _():
        for copy in upper + lower_on:
            copy.wait_send()


def finish(qf, qf_in, gate, gate_in, o_w, o_w_in, kmix, mixed, key_mixed, out_v, sem):
    rows = qf.shape[0]
    out_keys = pltpu.make_async_copy(kmix, key_mixed, sem.at[0])
    out_keys.start()
    outs = []
    steps = 2
    span = rows // steps
    pairs, _, deep = gate.shape
    for b in range(steps):
        r = slice(b * span, (b + 1) * span)
        total = None
        for feats, door, w in ((qf, gate, o_w), (qf_in, gate_in, o_w_in)):
            att = []
            for p in range(pairs):
                got = mm_nt(feats[r, p * deep : (p + 1) * deep], door[p])
                att.append((got[:, :LANES] / got[:, LANES:]).astype(BF16))
            got = mm(jnp.concatenate(att, axis=1), w[...])
            total = got if total is None else total + got
        out_v[r, :] = total.astype(BF16)
        piece = pl.ds(b * span, span)
        outs.append(pltpu.make_async_copy(out_v.at[piece, :], mixed.at[piece, :], sem.at[1 + b]))
        outs[b].start()
    out_keys.wait()
    for copy in outs:
        copy.wait()


def body(n, tokens, w_query, w_key, w_value, w_out, feature_dirs, kernel_taps):
    rows, half = tokens.shape
    d = w_key.shape[0]
    width = w_key.shape[1]
    heads = width // HEAD_DIM
    features = feature_dirs.shape[1]
    reach = (kernel_taps.shape[1] - 1) // 2
    block = 2 * reach
    out_cols = w_out.shape[1] // 2
    outer = n // heads
    chunk = HEAD_DIM + PAD
    vmem = pltpu.VMEM
    dma = pltpu.SemaphoreType.DMA
    any_spec = pl.BlockSpec(memory_space=pl.ANY)
    vmem_spec = pl.BlockSpec(memory_space=pltpu.VMEM)
    held = pl.pallas_call(
        functools.partial(fused, n, heads, reach),
        out_shape=(
            vmem((rows, heads * features), BF16),
            vmem((rows, heads * features), BF16),
            vmem((width // LANES, 2 * LANES, 2 * features), BF16),
            vmem((width // LANES, 2 * LANES, 2 * features), BF16),
            vmem((width, out_cols), BF16),
            vmem((width, out_cols), BF16),
            vmem((rows, width), BF16),
        ),
        in_specs=[any_spec] * 7,
        out_specs=(vmem_spec,) * 7,
        scratch_shapes=[
            vmem((rows + 2 * reach, d), BF16),
            vmem((d, width), BF16),
            vmem((d, width), BF16),
            vmem((d, width), BF16),
            vmem(feature_dirs.shape, F32),
            vmem(kernel_taps.shape, BF16),
            vmem((8, 2 * block), F32),
            vmem((heads * block, 2 * block), BF16),
            vmem((width, heads * features), BF16),
            vmem((width, heads * features), BF16),
            vmem((width, heads * features), BF16),
            vmem((rows + 2 * reach, width), BF16),
            vmem((heads, chunk, rows), BF16),
            vmem((rows, width), BF16),
            vmem((heads, chunk, features), F32),
            vmem((heads, chunk, features), BF16),
            vmem((heads - 1, chunk, features), BF16),
            vmem((chunk, features), BF16),
            vmem((outer, chunk, features), BF16),
            vmem((heads, chunk, features), BF16),
            vmem((heads, chunk, features), BF16),
            dma((7,)),
            dma((12,)),
            dma((12,)),
            dma((1, heads - 1)),
            dma((1, heads - 1)),
            dma((1, max(outer - 1, 1))),
            dma((1, outer)),
            dma((1, 2 * heads - 1)),
            dma((1, 2 * heads - 1)),
        ],
        compiler_params=pltpu.CompilerParams(collective_id=0, has_side_effects=True),
        name="fused",
    )(tokens, w_query, w_key, w_value, w_out, feature_dirs, kernel_taps)
    return pl.pallas_call(
        finish,
        out_shape=(
            jax.ShapeDtypeStruct((rows, out_cols), BF16),
            jax.ShapeDtypeStruct((rows, width), BF16),
        ),
        in_specs=[vmem_spec] * 7,
        out_specs=(any_spec, any_spec),
        scratch_shapes=[vmem((rows, out_cols), BF16), dma((3,))],
        name="finish",
    )(*[pltpu.with_memory_space_constraint(a, pltpu.VMEM) for a in held])


def solution(mesh):
    return jax.shard_map(
        functools.partial(body, mesh.shape["seq"]),
        mesh=mesh,
        in_specs=(
            P("seq", "head"),
            P(None, "head"),
            P(None, "head"),
            P(None, "head"),
            P("head", None),
            P(),
            P("head", None),
        ),
        out_specs=(P("seq", "head"), P("seq", "head")),
        check_vma=False,
    )
```
